512 devices in a mesh: blk: 512 (over y, x, z, core).
Axes of the slice: x: 4, y: 8, z: 8, core: 2. Of those that a mesh axis runs over, the one named last changes fastest.
Arguments:
- concentration: float32 [1536, 4, 40, 1024], P('blk'), may hold values from 0.2 to 2
- potential_guess: float32 [1536, 40, 1024], P('blk'), may hold values from -3 to 3
- diffusivity: float32 [4], replicated, may hold values from 0.5 to 2
- block_rows: int32 [1536], P('blk'), may hold values from 20 to 40, as said below
- block_home: int32 [1536], replicated, may hold values from 0 to 1535, as said below
- face_match: int32 [1536, 2, 3], P('blk'), may hold values from -1 to 1535, as said below
Outputs:
- species_end: float32 [1536, 4, 40, 1024], P('blk')
- potential: float32 [1536, 40, 1024], P('blk')
The draws below stay inside these ranges and needn't reach their ends.
Inputs may be any that keep to these rules, and one draw needn't show every extreme that they name: `block_rows`: the first block of every device has 40 live rows. `block_home`: A permutation of the block positions. `face_match`: matching is symmetric: a face's partner names it back with the same reverse flag, walls come in pairs of such faces. Every partner block lies on the same device as the face or on the device whose index is one higher or lower, cyclically over all devices; between two cyclically consecutive devices there is at most one matched (or wall-paired) face pair.
All inputs are finite; a program needn't handle non-finite values.
Results may differ from the reference program's by a relative error of at most 0.00002.
Values sent between devices are 32-bit elements; how exact they have to be, the bound alone decides.
No kernel may reach another device: no remote copies, remote signals or barrier semaphores. Data moves between devices by JAX's collectives and lax.ppermute only.
A program may use at most 128 MiB of HBM per device.

```python
import math
import jax
import jax.numpy as jnp

BLOCKS_DEV = 3
ROWS = 40
FACE = 1024
SWEEPS = 4
BLOCKS = 1536


def match_tables(key):
    total = BLOCKS
    devices = BLOCKS // BLOCKS_DEV
    per_device = 2 * BLOCKS_DEV
    home = jax.random.permutation(jax.random.fold_in(key, 11), total).astype(jnp.int32)
    identity = jnp.argsort(home).astype(jnp.int32)
    scores = jax.random.randint(jax.random.fold_in(key, 12), (devices, per_device), 0, 2 ** 20)
    scores = scores * per_device + jnp.arange(per_device, dtype=jnp.int32)[None, :]
    local_order = jnp.argsort(scores, axis=1).astype(jnp.int32)
    sequence = (jnp.arange(devices, dtype=jnp.int32)[:, None] * per_device + local_order).reshape(-1)
    places = jnp.arange(2 * total, dtype=jnp.int32)
    partner_place = jnp.where(places % 2 == 1, places + 1, places - 1) % (2 * total)
    pair_id = (places + 1) // 2 % total
    wall_pair = (jax.random.randint(jax.random.fold_in(key, 13), (total,), 0, 8) == 0).astype(jnp.int32)
    reverse_pair = jax.random.randint(jax.random.fold_in(key, 14), (total,), 0, 2).astype(jnp.int32)
    partner_face_id = jnp.zeros((2 * total,), jnp.int32).at[sequence].set(sequence[partner_place])
    wall_face = jnp.zeros((2 * total,), jnp.int32).at[sequence].set(wall_pair[pair_id])
    reverse_face = jnp.zeros((2 * total,), jnp.int32).at[sequence].set(reverse_pair[pair_id])
    partner_id = jnp.where(wall_face == 1, -1, identity[partner_face_id // 2])
    partner_side = jnp.where(wall_face == 1, 0, partner_face_id % 2)
    reverse_flag = jnp.where(wall_face == 1, 0, reverse_face)
    match = jnp.stack([partner_id, partner_side, reverse_flag], axis=-1).reshape(total, 2, 3)
    return (home, match.astype(jnp.int32))


def draw_block_home(key, part):
    home, match = match_tables(key)
    return home


def draw_face_match(key, part):
    home, match = match_tables(key)
    return match


def draw_block_rows(key, part):
    values = jax.random.randint(jax.random.fold_in(key, 21), (BLOCKS,), ROWS // 2, ROWS + 1).astype(jnp.int32)
    first_slot = jnp.arange(BLOCKS, dtype=jnp.int32) % BLOCKS_DEV == 0
    return jnp.where(first_slot, ROWS, values).astype(jnp.int32)


def levels(rng, shape, cuts, low, largest):
    gain = 1.0
    for position, blocks in cuts:
        heights = jax.random.uniform(jax.random.fold_in(jax.random.fold_in(rng, 6), position), (blocks,), jnp.float32, low / len(cuts), largest / len(cuts))
        gain = gain * jnp.repeat(jnp.exp(heights), shape[position] // blocks).reshape((-1,) + (1,) * (len(shape) - 1 - position))
    return gain


def gaussian(own_key, shape, spread, limit, shards=(), kind=jnp.bfloat16):
    loudness = levels(own_key, shape, shards, -0.22, 0.18) if shards else 1.0
    values = jax.random.normal(own_key, shape, jnp.float32) * spread * loudness
    return jnp.minimum(jnp.maximum(values, -limit), limit).astype(kind)


def setup_inputs(seed: int = 0) -> dict:
    seeds = jax.random.split(jax.random.key(seed), 7)
    concentration = jnp.clip(jnp.exp(math.log(2.0) - 2.3025851 * jax.random.uniform(seeds[0], (BLOCKS, 4, ROWS, FACE), jnp.float32) ** levels(seeds[0], (BLOCKS, 4, ROWS, FACE), ((0, 512),), -0.2, 0.2)), 0.2, 2.0)
    potential_guess = gaussian(seeds[1], (BLOCKS, ROWS, FACE), 0.5, 3.0, ((0, 512),), jnp.float32)
    diffusivity = jnp.clip(jnp.exp(jax.random.uniform(seeds[2], (4,), jnp.float32, math.log(0.5), math.log(2.0))), 0.5, 2.0)
    block_rows = draw_block_rows(jax.random.fold_in(seeds[6], 71), 0)
    block_home = draw_block_home(jax.random.fold_in(seeds[6], 71), 0)
    face_match = draw_face_match(jax.random.fold_in(seeds[6], 71), 0)
    return dict(concentration=concentration, potential_guess=potential_guess, diffusivity=diffusivity, block_rows=block_rows, block_home=block_home, face_match=face_match)


screening = 0.5
time_step = 0.1
smoother_weight = 0.8
coarse_weight = 0.8
valences = (1.0, -1.0, 2.0, -1.0)


def face_rows_of(values, top_mask):
    south_side = values[:, :, 0, :]
    north_side = jnp.sum(values * top_mask[:, None, :, None], axis=2)
    return jnp.stack([south_side, north_side], axis=1)


def orient_ghosts(picked, face_match):
    reverse_flag = (face_match[:, :, 2] == 1)[:, :, None, None]
    flipped = jnp.where(reverse_flag, picked[..., ::-1], picked)
    is_open = (face_match[:, :, 0] >= 0)[:, :, None, None]
    return jnp.where(is_open, flipped, jnp.zeros_like(flipped))


def partner_position(face_match, block_home):
    partner_id = jnp.maximum(face_match[:, :, 0], 0)
    return block_home[partner_id].astype(jnp.int32)


def link_masks(block_rows, face_match):
    row_index = jnp.arange(ROWS, dtype=jnp.int32)[None, :]
    col_index = jnp.arange(FACE, dtype=jnp.int32)
    live_rows = block_rows[:, None]
    alive_mask = row_index < live_rows
    top_row = row_index == live_rows - 1
    south_open = (face_match[:, 0, 0] >= 0)[:, None]
    north_open = (face_match[:, 1, 0] >= 0)[:, None]
    up_link = alive_mask & ((row_index + 1 < live_rows) | (top_row & north_open))
    down_link = alive_mask & ((row_index > 0) | south_open)
    up_link = up_link.astype(jnp.float32)[:, None, :, None]
    down_link = down_link.astype(jnp.float32)[:, None, :, None]
    left_link = (alive_mask[:, None, :, None] & (col_index > 0)[None, None, None, :]).astype(jnp.float32)
    right_link = (alive_mask[:, None, :, None] & (col_index < FACE - 1)[None, None, None, :]).astype(jnp.float32)
    alive_float = alive_mask.astype(jnp.float32)[:, None, :, None]
    return alive_float, top_row.astype(jnp.float32), (up_link, down_link, left_link, right_link)


def neighbor_values(values, ghosts, top_mask):
    zero_row = jnp.zeros_like(values[:, :, :1, :])
    first_row = (jnp.arange(ROWS, dtype=jnp.int32) == 0)[None, None, :, None]
    above_vals = jnp.concatenate([values[:, :, 1:, :], zero_row], axis=2)
    above_vals = jnp.where(top_mask[:, None, :, None] > 0, ghosts[:, 1][:, :, None, :], above_vals)
    below_vals = jnp.concatenate([zero_row, values[:, :, :-1, :]], axis=2)
    below_vals = jnp.where(first_row, ghosts[:, 0][:, :, None, :], below_vals)
    zero_col = jnp.zeros_like(values[..., :1])
    leftward = jnp.concatenate([zero_col, values[..., :-1]], axis=-1)
    rightward = jnp.concatenate([values[..., 1:], zero_col], axis=-1)
    return (above_vals, below_vals, leftward, rightward)


def apply_operator(values, neighbors, link_set):
    result = screening * values
    for link_mask, other in zip(link_set, neighbors):
        result = result + link_mask * (values - other)
    return result


def transport_rate(species, potential, species_nb, potential_nb, link_set, diffusivity):
    valence_col = jnp.array(valences, dtype=jnp.float32)[None, :, None, None]
    rate_sum = jnp.zeros_like(species)
    for link_mask, other, other_pot in zip(link_set, species_nb, potential_nb):
        rate_sum = rate_sum + link_mask * ((other - species) + valence_col * 0.5 * (species + other) * (other_pot - potential))
    return diffusivity[None, :, None, None] * rate_sum


def reference(concentration, potential_guess, diffusivity, block_rows, block_home, face_match):
    alive_float, top_mask, link_set = link_masks(block_rows, face_match)
    positions = partner_position(face_match, block_home)
    face_index = positions * 2 + face_match[:, :, 1]
    valence_col = jnp.array(valences, dtype=jnp.float32)[None, :, None, None]
    species_start = concentration * alive_float
    charge = jnp.sum(species_start * valence_col, axis=1, keepdims=True)
    guess = potential_guess[:, None] * alive_float
    diagonal = screening + link_set[0] + link_set[1] + link_set[2] + link_set[3]

    def ghosts_of(values):
        rows_out = face_rows_of(values, top_mask)
        flat_table = rows_out.reshape((-1,) + rows_out.shape[2:])
        return orient_ghosts(flat_table[face_index], face_match)

    def smooth(values):
        neighbors = neighbor_values(values, ghosts_of(values), top_mask)
        return values + smoother_weight * (charge - apply_operator(values, neighbors, link_set)) / diagonal

    smoothed = smooth(guess)
    residual = charge - apply_operator(smoothed, neighbor_values(smoothed, ghosts_of(smoothed), top_mask), link_set)
    block_residual = jnp.sum(residual, axis=(1, 2, 3))
    open_south = (face_match[:, 0, 0] >= 0).astype(jnp.float32)
    open_north = (face_match[:, 1, 0] >= 0).astype(jnp.float32)
    coarse_diag = screening * (block_rows.astype(jnp.float32) * FACE) + FACE * (open_south + open_north)
    correction = jnp.zeros_like(block_residual)
    for step_index in range(SWEEPS):
        neighbor_sum = open_south * correction[positions[:, 0]] + open_north * correction[positions[:, 1]]
        correction = correction + coarse_weight * (block_residual - (coarse_diag * correction - FACE * neighbor_sum)) / coarse_diag
    corrected = smoothed + correction[:, None, None, None] * alive_float
    potential = smooth(corrected)
    potential_nb = neighbor_values(potential, ghosts_of(potential), top_mask)

    def rate_of(species):
        species_nb = neighbor_values(species, ghosts_of(species), top_mask)
        return transport_rate(species, potential, species_nb, potential_nb, link_set, diffusivity)

    species_mid = species_start + time_step * rate_of(species_start)
    species_end = 0.5 * species_start + 0.5 * (species_mid + time_step * rate_of(species_mid))
    return species_end, potential[:, 0]
```

```python
import functools

import jax
import jax.numpy as jnp
from jax import lax
from jax.experimental import pallas as pl
from jax.experimental.pallas import tpu as pltpu
from jax.sharding import PartitionSpec as P

AXIS = "blk"
B, S, ROWS, FACE = 3, 4, 40, 1024
NT = FACE // 128
LO = 8
H = 56
NI = 6
VALENCES = (1.0, -1.0, 2.0, -1.0)
W_IN, W_EDGE = 0.8 / 4.5, 0.8 / 3.5
WALL = -1000.0
MID = 18
F32 = jnp.float32


def face_info(match_s, home_s, b, side, me, devices):
    g = match_s[b, side, 0]
    pos = home_s[jnp.maximum(g, 0)]
    dev = lax.div(pos, jnp.int32(B))
    pb = pos - dev * B
    off = lax.rem(dev - me + 1 + devices, devices)
    return g >= 0, off, pb, match_s[b, side, 1], match_s[b, side, 2], (off - 1) * B + pb - b


def iota(shape, dim):
    return lax.broadcasted_iota(jnp.int32, shape, dim)


def pack_kernel(devices, conc, pot, rows_s, home_s, match_s, strips, msg_e, msg_o, U, G, Q, sem):
    me = lax.axis_index(AXIS)
    core = lax.rem(me, 2)

    def copies(b):
        out = []
        for j in range(NT):
            cols = pl.ds(128 * j, 128)
            out.append(pltpu.make_async_copy(conc.at[b, :, :, cols], U.at[b, :, j, pl.ds(LO, ROWS), :], sem.at[b]))
            out.append(pltpu.make_async_copy(pot.at[b, :, cols], G.at[b, j, pl.ds(LO, ROWS), :], sem.at[b]))
        return out

    for b in range(B):
        for c in copies(b):
            c.start()

    rowid = iota((ROWS, 128), 0)
    lane = iota((ROWS, 128), 1)
    first, last = lane == 0, lane == 127
    zero = jnp.zeros((ROWS, 128), F32)
    l8, s8 = iota((8, 128), 1), iota((8, 128), 0)
    mirror = 127 - l8

    def block(b, carry):
        W, fe, fo = carry
        for c in copies(b):
            c.wait()
        n = rows_s[b]
        info = [face_info(match_s, home_s, b, side, me, devices) for side in range(2)]
        live = rowid < n
        pad = jnp.zeros((8, 128), F32)
        for j in range(NT):
            c = [U[b, s, j, LO : LO + ROWS, :] for s in range(S)]
            q = c[0] - c[1] + 2.0 * c[2] - c[3]
            Q[b, j, LO : LO + ROWS, :] = jnp.where(live, q, 0.0)
            G[b, j, LO : LO + ROWS, :] = jnp.where(live, G[b, j, LO : LO + ROWS, :], 0.0)
            G[b, j, 0:LO, :] = pad
            G[b, j, LO + ROWS : H, :] = pad
        op = [i[0].astype(F32) for i in info]
        links = (
            2.0
            - jnp.where(rowid == 0, 1.0 - op[0], 0.0)
            - jnp.where(rowid == n - 1, 1.0 - op[1], 0.0)
        )
        w_in = jnp.where(live, 0.8 / (2.5 + links), 0.0)
        w_edge = jnp.where(live, 0.8 / (1.5 + links), 0.0)
        g = [G[b, j, LO : LO + ROWS, :] for j in range(NT)]
        gr = [pltpu.roll(x, 1, 1) for x in g]
        gl = [pltpu.roll(x, 127, 1) for x in g]
        total = s_sum = t_sum = zero
        for j in range(NT):
            left = jnp.where(first, gr[j - 1] if j else zero, gr[j])
            right = jnp.where(last, gl[j + 1] if j < NT - 1 else zero, gl[j])
            near = (
                G[b, j, LO + 1 : LO + 1 + ROWS, :] + G[b, j, LO - 1 : LO - 1 + ROWS, :] + left + right
            )
            w, wf = w_in, W_IN
            if j in (0, NT - 1):
                edge = first if j == 0 else last
                w, wf = jnp.where(edge, w_edge, w_in), jnp.where(edge, W_EDGE, W_IN)
            q = Q[b, j, LO : LO + ROWS, :]
            sm = 0.2 * g[j] + w * (q + near)
            total += q - 0.5 * sm
            s_sum += sm
            t_sum += wf * g[j]
        own = t_sum - s_sum
        away = s_sum - 1.5 * t_sum
        ends = [rowid == 0, rowid == n - 1]
        total += jnp.where(ends[0], op[0] * own, 0.0) + jnp.where(ends[1], op[1] * own, 0.0)
        vals = [jnp.sum(total, keepdims=True)]
        vals.append(1.0 / jnp.full((1, 1), 512.0 * n.astype(F32) + 1024.0 * (op[0] + op[1]), F32))
        vals += [jnp.sum(jnp.where(e, away, 0.0), keepdims=True) for e in ends]
        vals += [
            jnp.full((1, 1), jnp.where(i[0], i[5].astype(F32), WALL), F32) for i in info
        ]
        col = jnp.zeros((8, 128), F32)
        for k, v in enumerate(vals):
            col = jnp.where(s8 == k, v, col)
        W = jnp.where(l8 == MID + B * core + b, col, W)
        for side in range(2):
            f = 2 * b + side
            is_open, off, _, _, rev, _ = info[side]
            even = is_open & (off == 2 - 2 * core)
            odd = is_open & (off == 2 * core)
            fe, fo = jnp.where(even, f, fe), jnp.where(odd, f, fo)
            for k in range(4):
                row = LO + k if side == 0 else LO + n - 1 - k
                at = pl.ds(row, 1)
                strips[f, :, k : k + 1, :] = G[b, :, at, :]
                if k < 3:
                    strips[f, :, 4 + k : 5 + k, :] = Q[b, :, at, :]
                if k < 2:
                    for s in range(S):
                        strips[f, :, 7 + 2 * s + k : 8 + 2 * s + k, :] = U[b, s, :, at, :]

            @pl.when(rev == 1)
            def _():
                for j in range(NT // 2):
                    for h in range(0, 16, 8):
                        x = strips[f, j, h : h + 8, :]
                        y = strips[f, NT - 1 - j, h : h + 8, :]
                        strips[f, j, h : h + 8, :] = jnp.take_along_axis(y, mirror, axis=1)
                        strips[f, NT - 1 - j, h : h + 8, :] = jnp.take_along_axis(x, mirror, axis=1)

        return W, fe, fo

    for f in range(2 * B):
        strips[f, :, 15:16, :] = jnp.zeros((NT, 1, 128), F32)
    W, fe, fo = lax.fori_loop(
        0, B, block, (jnp.zeros((8, 128), F32), jnp.int32(0), jnp.int32(0))
    )
    for msg, f in ((msg_e, fe), (msg_o, fo)):
        for j in range(NT):
            msg[j] = strips[f, j]
        msg[NT, 0:8, :] = W
        msg[NT, 8:16, :] = jnp.zeros((8, 128), F32)


def turn(x, shift, core):
    return jnp.where(core == 1, pltpu.roll(x, shift, 1), pltpu.roll(x, 128 - shift, 1))


def chip_kernel(mine, theirs, out):
    out[0] = mine[0] + theirs[0]


def pair_kernel(mine, theirs, out):
    core = lax.rem(lax.axis_index(AXIS), 2)
    out[...] = mine[0] + turn(theirs[0], 6, core)


def far_kernel(mine, theirs, out):
    core = lax.rem(lax.axis_index(AXIS), 2)
    out[...] = mine[...] + turn(theirs[...], 12, core)


def coarse(W):
    n = 48
    I, J = iota((n, 128), 0).astype(F32), iota((n, 128), 1).astype(F32)
    lane = J[0:1]
    Wt = jnp.transpose(jnp.concatenate([W, jnp.zeros((120, 128), F32)], axis=0))[0:n]
    row = [W[k : k + 1] for k in range(6)]
    col = [Wt[:, k : k + 1] for k in range(6)]
    to = [(col[4 + s] + I) == J for s in range(2)]
    fro = [(row[4 + s] + lane) == I for s in range(2)]
    r_row = row[0] + jnp.sum(
        jnp.where(to[0], col[2], 0.0) + jnp.where(to[1], col[3], 0.0), axis=0, keepdims=True
    )
    r_col = col[0] + jnp.sum(
        jnp.where(fro[0], row[2], 0.0) + jnp.where(fro[1], row[3], 0.0), axis=1, keepdims=True
    )
    links = to[0].astype(F32) + to[1].astype(F32)
    diag = jnp.where(I == J, 0.2, 0.0)
    g_row, g_col = 0.8 * r_row * row[1], 0.8 * r_col * col[1]
    m_row = links * (819.2 * row[1]) + diag
    m_col = links * (819.2 * col[1]) + diag
    x = g_col
    x = g_row + jnp.sum(m_row * x, axis=0, keepdims=True)
    x = g_col + jnp.sum(m_col * x, axis=1, keepdims=True)
    return g_row + jnp.sum(m_row * x, axis=0, keepdims=True)


def main_kernel(
    devices, conc, pot, strips, got_e, got_o, w_mine, w_theirs, rows_s, home_s, match_s, diff_s,
    end_out, pot_out, U, G, Q, ST, DV, DH, MIDS, CR, sem, st_sem, out_sem,
):
    me = lax.axis_index(AXIS)
    core = lax.rem(me, 2)

    def copies(b):
        out = []
        for j in range(NT):
            cols = pl.ds(128 * j, 128)
            out.append(pltpu.make_async_copy(conc.at[b, :, :, cols], U.at[b, :, j, pl.ds(LO, ROWS), :], sem.at[b]))
            out.append(pltpu.make_async_copy(pot.at[b, :, cols], G.at[b, j, pl.ds(LO, ROWS), :], sem.at[b]))
        return out

    def results(b):
        out = []
        for j in range(NT):
            cols = pl.ds(128 * j, 128)
            out.append(pltpu.make_async_copy(U.at[b, :, j, pl.ds(LO, ROWS), :], end_out.at[b, :, :, cols], out_sem.at[b]))
            out.append(pltpu.make_async_copy(G.at[b, j, pl.ds(LO, ROWS), :], pot_out.at[b, :, cols], out_sem.at[b]))
        return out

    halo = [
        pltpu.make_async_copy(strips, ST.at[pl.ds(0, 6)], st_sem.at[0]),
        pltpu.make_async_copy(got_e.at[pl.ds(0, NT)], ST.at[6], st_sem.at[1]),
        pltpu.make_async_copy(got_o.at[pl.ds(0, NT)], ST.at[7], st_sem.at[2]),
    ]
    for c in halo:
        c.start()
    for b in range(B):
        for c in copies(b):
            c.start()

    l8, s8 = iota((8, 128), 1), iota((8, 128), 0)
    in_chip = (l8 >= MID) & (l8 < MID + 6)
    W = w_mine[...] + jnp.where(in_chip, 0.0, w_theirs[...])
    CR[...] = jnp.broadcast_to(coarse(W), (8, 128))
    for c in halo:
        c.wait()

    rowid = iota((ROWS, 128), 0)
    first, last = l8 == 0, l8 == 127
    zero = jnp.zeros((8, 128), F32)

    def at(i):
        return pl.ds(4 + i, 8, stride=NI)

    def up(x):
        return x[1:] + [pltpu.roll(x[0], 7, 0)]

    def down(x):
        return [pltpu.roll(x[NI - 1], 1, 0)] + x[:-1]

    def right_of(x, nxt):
        return [
            jnp.where(last, zero if nxt is None else pltpu.roll(nxt[i], 127, 1), pltpu.roll(x[i], 127, 1))
            for i in range(NI)
        ]

    def left_of(x, prv):
        return [
            jnp.where(first, zero if prv is None else pltpu.roll(prv[i], 1, 1), pltpu.roll(x[i], 1, 1))
            for i in range(NI)
        ]

    def block(b, _):
        for c in copies(b):
            c.wait()
        n = rows_s[b]
        info = [face_info(match_s, home_s, b, side, me, devices) for side in range(2)]
        live = rowid < n
        for j in range(NT):
            G[b, j, LO : LO + ROWS, :] = jnp.where(live, G[b, j, LO : LO + ROWS, :], 0.0)
            c = []
            for s in range(S):
                x = jnp.where(live, U[b, s, j, LO : LO + ROWS, :], 0.0)
                U[b, s, j, LO : LO + ROWS, :] = x
                U[b, s, j, 0:LO, :] = zero
                U[b, s, j, LO + ROWS : H, :] = zero
                c.append(x)
            Q[b, j, LO : LO + ROWS, :] = c[0] - c[1] + 2.0 * c[2] - c[3]
            for ref in (G, Q):
                ref[b, j, 0:LO, :] = zero
                ref[b, j, LO + ROWS : H, :] = zero
        for side in range(2):
            is_open, off, pb, pf, _, _ = info[side]
            src = jnp.where(off == 1, 2 * pb + pf, jnp.where(off == 2 - 2 * core, 6, 7))

            @pl.when(is_open)
            def _():
                for k in range(4):
                    row = pl.ds(LO - 1 - k if side == 0 else LO + n + k, 1)
                    G[b, :, row, :] = ST[src, :, k : k + 1, :]
                    if k < 3:
                        Q[b, :, row, :] = ST[src, :, 4 + k : 5 + k, :]
                    if k < 2:
                        for s in range(S):
                            U[b, s, :, row, :] = ST[src, :, 7 + 2 * s + k : 8 + 2 * s + k, :]

        lane_own = MID + B * core + b
        cr = CR[...]

        def pick(l):
            return jnp.sum(jnp.where(l8 == l, cr, 0.0), axis=1, keepdims=True)

        c_own = pick(lane_own)
        c_side = [pick(lane_own + i[5]) for i in info]
        lo = jnp.where(info[0][0], -4, 0)
        hi = jnp.where(info[1][0], n + 3, n - 1)
        w_in, w_edge, corr, alive, linked = [], [], [], [], []
        for i in range(NI):
            r = NI * s8 + (i - 4)
            inside = (r >= lo) & (r <= hi)
            wall = ((r == 0) & (lo == 0)) | ((r == n - 1) & (hi == n - 1))
            links = jnp.where(wall, 1.0, 2.0)
            w_in.append(jnp.where(inside, 0.8 / (2.5 + links), 0.0))
            w_edge.append(jnp.where(inside, 0.8 / (1.5 + links), 0.0))
            c = jnp.where(r < 0, c_side[0], jnp.where(r >= n, c_side[1], c_own))
            corr.append(jnp.where(inside, c, 0.0))
            alive.append((r >= 0) & (r < n))
            linked.append(jnp.logical_not(((r == -1) & (lo == 0)) | ((r == n - 1) & (hi == n - 1))))

        def weight(i, j):
            if j == 0:
                return jnp.where(first, w_edge[i], w_in[i])
            if j == NT - 1:
                return jnp.where(last, w_edge[i], w_in[i])
            return w_in[i]

        def smooth(load, store):
            prv, cur = None, [load(i, 0) for i in range(NI)]
            for j in range(NT):
                nxt = [load(i, j + 1) for i in range(NI)] if j < NT - 1 else None
                u, d, lf, rt = up(cur), down(cur), left_of(cur, prv), right_of(cur, nxt)
                for i in range(NI):
                    q = Q[b, j, at(i), :]
                    store(i, j, 0.2 * cur[i] + weight(i, j) * (q + ((u[i] + d[i]) + (lf[i] + rt[i]))))
                prv, cur = cur, nxt

        def put_v(i, j, x):
            MIDS[i, j] = x + corr[i]

        def put_phi(i, j, x):
            DV[i, j] = x

        smooth(lambda i, j: G[b, j, at(i), :], put_v)
        smooth(lambda i, j: MIDS[i, j], put_phi)
        cur = [DV[i, 0] for i in range(NI)]
        for j in range(NT):
            nxt = [DV[i, j + 1] for i in range(NI)] if j < NT - 1 else None
            u, rt = up(cur), right_of(cur, nxt)
            for i in range(NI):
                G[b, j, at(i), :] = jnp.where(alive[i], cur[i], 0.0)
                DV[i, j] = u[i] - cur[i]
                DH[i, j] = rt[i] - cur[i]
            cur = nxt

        def species(s, _):
            half_z = jnp.where(s == 0, 0.5, jnp.where(s == 2, 1.0, -0.5)).astype(F32)
            k1 = 0.1 * diff_s[s]

            def stage(load, store):
                prv, cur = None, [load(i, 0) for i in range(NI)]
                for j in range(NT):
                    nxt = [load(i, j + 1) for i in range(NI)] if j < NT - 1 else None
                    u, rt = up(cur), right_of(cur, nxt)
                    fv, fh = [], []
                    for i in range(NI):
                        f = (u[i] - cur[i]) + (u[i] + cur[i]) * (half_z * DV[i, j])
                        fv.append(jnp.where(linked[i], f, 0.0))
                        f = (rt[i] - cur[i]) + (rt[i] + cur[i]) * (half_z * DH[i, j])
                        fh.append(jnp.where(last, 0.0, f) if j == NT - 1 else f)
                    fd, fl = down(fv), left_of(fh, prv)
                    for i in range(NI):
                        store(i, j, cur[i], (fv[i] - fd[i]) + (fh[i] - fl[i]))
                    prv, cur = fh, nxt

            def put_mid(i, j, u, rate):
                MIDS[i, j] = u + k1 * rate

            def put_end(i, j, mid, rate):
                u = U[b, s, j, at(i), :]
                x = 0.5 * u + 0.5 * (mid + k1 * rate)
                U[b, s, j, at(i), :] = jnp.where(alive[i], x, 0.0)

            stage(lambda i, j: U[b, s, j, at(i), :], put_mid)
            stage(lambda i, j: MIDS[i, j], put_end)
            return 0

        lax.fori_loop(0, S, species, 0)
        for c in results(b):
            c.start()
        return 0

    lax.fori_loop(0, B, block, 0)
    for b in range(B):
        for c in results(b):
            c.wait()


ANY = pl.BlockSpec(memory_space=pl.ANY)
SMEM = pl.BlockSpec(memory_space=pltpu.SMEM)
VMEM = pl.BlockSpec(memory_space=pltpu.VMEM)
PARAMS = pltpu.CompilerParams(vmem_limit_bytes=40 * 1024 * 1024)


def shaped(*shape):
    return jax.ShapeDtypeStruct(shape, F32)


def body(concentration, potential_guess, diffusivity, block_rows, block_home, face_match):
    devices = lax.axis_size(AXIS)

    def swap(x, pairs):
        return lax.ppermute(x, AXIS, pairs)

    on_chip = [(i, i ^ 1) for i in range(devices)]
    off_chip = [(i, (i + 1 if i % 2 else i - 1) % devices) for i in range(devices)]
    beyond = [((i + 4 if i % 2 else i - 4) % devices, i) for i in range(devices)]

    strips, msg_e, msg_o = pl.pallas_call(
        functools.partial(pack_kernel, devices),
        out_shape=(shaped(2 * B, NT, 16, 128), shaped(NT + 1, 16, 128), shaped(NT + 1, 16, 128)),
        in_specs=[ANY, ANY, SMEM, SMEM, SMEM],
        out_specs=(VMEM, VMEM, VMEM),
        scratch_shapes=[
            pltpu.VMEM((B, S, NT, H, 128), F32),
            pltpu.VMEM((B, NT, H, 128), F32),
            pltpu.VMEM((B, NT, H, 128), F32),
            pltpu.SemaphoreType.DMA((B,)),
        ],
        compiler_params=PARAMS,
        name="pack",
    )(concentration, potential_guess, block_rows, block_home, face_match)

    got_e = swap(msg_e, on_chip)
    record = pl.BlockSpec((1, 8, 128), lambda i: (NT, 0, 0))
    whole = pl.BlockSpec((8, 128), lambda i: (0, 0))
    msg_o = pl.pallas_call(
        chip_kernel,
        grid=(1,),
        out_shape=shaped(NT + 1, 16, 128),
        in_specs=[record, record],
        out_specs=record,
        input_output_aliases={0: 0},
        name="chip",
    )(msg_o, got_e)
    got_o = swap(msg_o, off_chip)
    w1 = pl.pallas_call(
        pair_kernel,
        grid=(1,),
        out_shape=shaped(8, 128),
        in_specs=[record, record],
        out_specs=whole,
        name="pair",
    )(msg_o, got_o)
    w2 = pl.pallas_call(
        far_kernel,
        out_shape=shaped(8, 128),
        in_specs=[VMEM, VMEM],
        out_specs=VMEM,
        name="far",
    )(w1, swap(w1, beyond))
    w_other = swap(w2, on_chip)

    return pl.pallas_call(
        functools.partial(main_kernel, devices),
        out_shape=(shaped(B, S, ROWS, FACE), shaped(B, ROWS, FACE)),
        in_specs=[ANY] * 5 + [VMEM, VMEM] + [SMEM] * 4,
        out_specs=(ANY, ANY),
        scratch_shapes=[
            pltpu.VMEM((B, S, NT, H, 128), F32),
            pltpu.VMEM((B, NT, H, 128), F32),
            pltpu.VMEM((B, NT, H, 128), F32),
            pltpu.VMEM((8, NT, 16, 128), F32),
            pltpu.VMEM((NI, NT, 8, 128), F32),
            pltpu.VMEM((NI, NT, 8, 128), F32),
            pltpu.VMEM((NI, NT, 8, 128), F32),
            pltpu.VMEM((8, 128), F32),
            pltpu.SemaphoreType.DMA((B,)),
            pltpu.SemaphoreType.DMA((3,)),
            pltpu.SemaphoreType.DMA((B,)),
        ],
        compiler_params=PARAMS,
        name="transport",
    )(
        concentration, potential_guess, strips, got_e, got_o, w2, w_other,
        block_rows, block_home, face_match, diffusivity,
    )


def solution(mesh):
    in_specs = (
        P("blk", None, None, None),
        P("blk", None, None),
        P(),
        P("blk"),
        P(),
        P("blk", None, None),
    )
    out_specs = (P("blk", None, None, None), P("blk", None, None))
    return jax.shard_map(body, mesh=mesh, in_specs=in_specs, out_specs=out_specs, check_vma=False)
```

```python
import functools

import jax
import jax.numpy as jnp
from jax import lax
from jax.experimental import pallas as pl
from jax.experimental.pallas import tpu as pltpu
from jax.sharding import PartitionSpec as P

AXIS = "blk"
B, S, ROWS, FACE = 3, 4, 40, 1024
NT = FACE // 128
LO = 8
H = 56
NI = 6
VALENCES = (1.0, -1.0, 2.0, -1.0)
W_IN, W_EDGE = 0.8 / 4.5, 0.8 / 3.5
WALL = -1000.0
MID = 18
F32 = jnp.float32


def face_info(match_s, home_s, b, side, me, devices):
    g = match_s[b, side, 0]
    pos = home_s[jnp.maximum(g, 0)]
    dev = lax.div(pos, jnp.int32(B))
    pb = pos - dev * B
    off = lax.rem(dev - me + 1 + devices, devices)
    return g >= 0, off, pb, match_s[b, side, 1], match_s[b, side, 2], (off - 1) * B + pb - b


def iota(shape, dim):
    return lax.broadcasted_iota(jnp.int32, shape, dim)


def pack_kernel(
    devices, conc, pot, rows, home, match, strips, msg_e, msg_o,
    U, G, Q, rows_s, home_s, match_s, sem, tab_sem,
):
    me = lax.axis_index(AXIS)
    core = lax.rem(me, 2)

    def copies(b):
        out = []
        for j in range(NT):
            cols = pl.ds(128 * j, 128)
            out.append(pltpu.make_async_copy(conc.at[b, :, :, cols], U.at[b, :, j, pl.ds(LO, ROWS), :], sem.at[b]))
            out.append(pltpu.make_async_copy(pot.at[b, :, cols], G.at[b, j, pl.ds(LO, ROWS), :], sem.at[b]))
        return out

    tables = [
        pltpu.make_async_copy(src, dst, tab_sem.at[k])
        for k, (src, dst) in enumerate(((rows, rows_s), (home, home_s), (match, match_s)))
    ]
    for c in tables:
        c.start()
    for b in range(B):
        for c in copies(b):
            c.start()
    for c in tables:
        c.wait()

    rowid = iota((ROWS, 128), 0)
    lane = iota((ROWS, 128), 1)
    first, last = lane == 0, lane == 127
    zero = jnp.zeros((ROWS, 128), F32)
    l8, s8 = iota((8, 128), 1), iota((8, 128), 0)
    mirror = 127 - l8

    def block(b, carry):
        W, fe, fo = carry
        for c in copies(b):
            c.wait()
        n = rows_s[b]
        info = [face_info(match_s, home_s, b, side, me, devices) for side in range(2)]
        live = rowid < n
        pad = jnp.zeros((8, 128), F32)
        for j in range(NT):
            c = [U[b, s, j, LO : LO + ROWS, :] for s in range(S)]
            q = c[0] - c[1] + 2.0 * c[2] - c[3]
            Q[b, j, LO : LO + ROWS, :] = jnp.where(live, q, 0.0)
            G[b, j, LO : LO + ROWS, :] = jnp.where(live, G[b, j, LO : LO + ROWS, :], 0.0)
            G[b, j, 0:LO, :] = pad
            G[b, j, LO + ROWS : H, :] = pad
        op = [i[0].astype(F32) for i in info]
        links = (
            2.0
            - jnp.where(rowid == 0, 1.0 - op[0], 0.0)
            - jnp.where(rowid == n - 1, 1.0 - op[1], 0.0)
        )
        w_in = jnp.where(live, 0.8 / (2.5 + links), 0.0)
        w_edge = jnp.where(live, 0.8 / (1.5 + links), 0.0)
        g = [G[b, j, LO : LO + ROWS, :] for j in range(NT)]
        gr = [pltpu.roll(x, 1, 1) for x in g]
        gl = [pltpu.roll(x, 127, 1) for x in g]
        total = s_sum = t_sum = zero
        for j in range(NT):
            left = jnp.where(first, gr[j - 1] if j else zero, gr[j])
            right = jnp.where(last, gl[j + 1] if j < NT - 1 else zero, gl[j])
            near = (
                G[b, j, LO + 1 : LO + 1 + ROWS, :] + G[b, j, LO - 1 : LO - 1 + ROWS, :] + left + right
            )
            w, wf = w_in, W_IN
            if j in (0, NT - 1):
                edge = first if j == 0 else last
                w, wf = jnp.where(edge, w_edge, w_in), jnp.where(edge, W_EDGE, W_IN)
            q = Q[b, j, LO : LO + ROWS, :]
            sm = 0.2 * g[j] + w * (q + near)
            total += q - 0.5 * sm
            s_sum += sm
            t_sum += wf * g[j]
        own = t_sum - s_sum
        away = s_sum - 1.5 * t_sum
        ends = [rowid == 0, rowid == n - 1]
        total += jnp.where(ends[0], op[0] * own, 0.0) + jnp.where(ends[1], op[1] * own, 0.0)
        vals = [jnp.sum(total, keepdims=True)]
        vals.append(1.0 / jnp.full((1, 1), 512.0 * n.astype(F32) + 1024.0 * (op[0] + op[1]), F32))
        vals += [jnp.sum(jnp.where(e, away, 0.0), keepdims=True) for e in ends]
        vals += [
            jnp.full((1, 1), jnp.where(i[0], i[5].astype(F32), WALL), F32) for i in info
        ]
        col = jnp.zeros((8, 128), F32)
        for k, v in enumerate(vals):
            col = jnp.where(s8 == k, v, col)
        W = jnp.where(l8 == MID + B * core + b, col, W)
        for side in range(2):
            f = 2 * b + side
            is_open, off, _, _, rev, _ = info[side]
            even = is_open & (off == 2 - 2 * core)
            odd = is_open & (off == 2 * core)
            fe, fo = jnp.where(even, f, fe), jnp.where(odd, f, fo)
            for k in range(4):
                row = LO + k if side == 0 else LO + n - 1 - k
                at = pl.ds(row, 1)
                strips[f, :, k : k + 1, :] = G[b, :, at, :]
                if k < 3:
                    strips[f, :, 4 + k : 5 + k, :] = Q[b, :, at, :]
                if k < 2:
                    for s in range(S):
                        strips[f, :, 7 + 2 * s + k : 8 + 2 * s + k, :] = U[b, s, :, at, :]

            @pl.when(rev == 1)
            def _():
                for j in range(NT // 2):
                    for h in range(0, 16, 8):
                        x = strips[f, j, h : h + 8, :]
                        y = strips[f, NT - 1 - j, h : h + 8, :]
                        strips[f, j, h : h + 8, :] = jnp.take_along_axis(y, mirror, axis=1)
                        strips[f, NT - 1 - j, h : h + 8, :] = jnp.take_along_axis(x, mirror, axis=1)

        return W, fe, fo

    for f in range(2 * B):
        strips[f, :, 15:16, :] = jnp.zeros((NT, 1, 128), F32)
    W, fe, fo = lax.fori_loop(
        0, B, block, (jnp.zeros((8, 128), F32), jnp.int32(0), jnp.int32(0))
    )
    for msg, f in ((msg_e, fe), (msg_o, fo)):
        for j in range(NT):
            msg[j] = strips[f, j]
        msg[NT, 0:8, :] = W
        msg[NT, 8:16, :] = jnp.zeros((8, 128), F32)


def turn(x, shift, core):
    return jnp.where(core == 1, jnp.roll(x, shift, 1), jnp.roll(x, -shift, 1))


def coarse(W):
    n = 48
    I, J = iota((n, 128), 0).astype(F32), iota((n, 128), 1).astype(F32)
    lane = J[0:1]
    Wt = jnp.transpose(jnp.concatenate([W, jnp.zeros((120, 128), F32)], axis=0))[0:n]
    row = [W[k : k + 1] for k in range(6)]
    col = [Wt[:, k : k + 1] for k in range(6)]
    to = [(col[4 + s] + I) == J for s in range(2)]
    fro = [(row[4 + s] + lane) == I for s in range(2)]
    r_row = row[0] + jnp.sum(
        jnp.where(to[0], col[2], 0.0) + jnp.where(to[1], col[3], 0.0), axis=0, keepdims=True
    )
    r_col = col[0] + jnp.sum(
        jnp.where(fro[0], row[2], 0.0) + jnp.where(fro[1], row[3], 0.0), axis=1, keepdims=True
    )
    links = to[0].astype(F32) + to[1].astype(F32)
    diag = jnp.where(I == J, 0.2, 0.0)
    g_row, g_col = 0.8 * r_row * row[1], 0.8 * r_col * col[1]
    m_row = links * (819.2 * row[1]) + diag
    m_col = links * (819.2 * col[1]) + diag
    x = g_col
    x = g_row + jnp.sum(m_row * x, axis=0, keepdims=True)
    x = g_col + jnp.sum(m_col * x, axis=1, keepdims=True)
    return g_row + jnp.sum(m_row * x, axis=0, keepdims=True)


def main_kernel(
    devices, conc, pot, strips, got_e, got_o, w_mine, w_theirs, rows, home, match, diff,
    end_out, pot_out, U, G, Q, ST, DV, DH, MIDS, CR, rows_s, home_s, match_s, diff_s,
    sem, st_sem, out_sem, tab_sem,
):
    me = lax.axis_index(AXIS)
    core = lax.rem(me, 2)

    def copies(b):
        out = []
        for j in range(NT):
            cols = pl.ds(128 * j, 128)
            out.append(pltpu.make_async_copy(conc.at[b, :, :, cols], U.at[b, :, j, pl.ds(LO, ROWS), :], sem.at[b]))
            out.append(pltpu.make_async_copy(pot.at[b, :, cols], G.at[b, j, pl.ds(LO, ROWS), :], sem.at[b]))
        return out

    def results(b):
        out = []
        for j in range(NT):
            cols = pl.ds(128 * j, 128)
            out.append(pltpu.make_async_copy(U.at[b, :, j, pl.ds(LO, ROWS), :], end_out.at[b, :, :, cols], out_sem.at[b]))
            out.append(pltpu.make_async_copy(G.at[b, j, pl.ds(LO, ROWS), :], pot_out.at[b, :, cols], out_sem.at[b]))
        return out

    halo = [
        pltpu.make_async_copy(strips, ST.at[pl.ds(0, 6)], st_sem.at[0]),
        pltpu.make_async_copy(got_e.at[pl.ds(0, NT)], ST.at[6], st_sem.at[1]),
        pltpu.make_async_copy(got_o.at[pl.ds(0, NT)], ST.at[7], st_sem.at[2]),
    ]
    pairs = ((rows, rows_s), (home, home_s), (match, match_s), (diff, diff_s))
    tables = [
        pltpu.make_async_copy(src, dst, tab_sem.at[k]) for k, (src, dst) in enumerate(pairs)
    ]
    for c in tables + halo:
        c.start()
    for b in range(B):
        for c in copies(b):
            c.start()

    l8, s8 = iota((8, 128), 1), iota((8, 128), 0)
    in_chip = (l8 >= MID) & (l8 < MID + 6)
    W = w_mine[...] + jnp.where(in_chip, 0.0, w_theirs[...])
    CR[...] = jnp.broadcast_to(coarse(W), (8, 128))
    for c in tables + halo:
        c.wait()

    rowid = iota((ROWS, 128), 0)
    first, last = l8 == 0, l8 == 127
    zero = jnp.zeros((8, 128), F32)

    def at(i):
        return pl.ds(4 + i, 8, stride=NI)

    def up(x):
        return x[1:] + [pltpu.roll(x[0], 7, 0)]

    def down(x):
        return [pltpu.roll(x[NI - 1], 1, 0)] + x[:-1]

    def right_of(x, nxt):
        return [
            jnp.where(last, zero if nxt is None else pltpu.roll(nxt[i], 127, 1), pltpu.roll(x[i], 127, 1))
            for i in range(NI)
        ]

    def left_of(x, prv):
        return [
            jnp.where(first, zero if prv is None else pltpu.roll(prv[i], 1, 1), pltpu.roll(x[i], 1, 1))
            for i in range(NI)
        ]

    def block(b, _):
        for c in copies(b):
            c.wait()
        n = rows_s[b]
        info = [face_info(match_s, home_s, b, side, me, devices) for side in range(2)]
        live = rowid < n
        for j in range(NT):
            G[b, j, LO : LO + ROWS, :] = jnp.where(live, G[b, j, LO : LO + ROWS, :], 0.0)
            c = []
            for s in range(S):
                x = jnp.where(live, U[b, s, j, LO : LO + ROWS, :], 0.0)
                U[b, s, j, LO : LO + ROWS, :] = x
                U[b, s, j, 0:LO, :] = zero
                U[b, s, j, LO + ROWS : H, :] = zero
                c.append(x)
            Q[b, j, LO : LO + ROWS, :] = c[0] - c[1] + 2.0 * c[2] - c[3]
            for ref in (G, Q):
                ref[b, j, 0:LO, :] = zero
                ref[b, j, LO + ROWS : H, :] = zero
        for side in range(2):
            is_open, off, pb, pf, _, _ = info[side]
            src = jnp.where(off == 1, 2 * pb + pf, jnp.where(off == 2 - 2 * core, 6, 7))

            @pl.when(is_open)
            def _():
                for k in range(4):
                    row = pl.ds(LO - 1 - k if side == 0 else LO + n + k, 1)
                    G[b, :, row, :] = ST[src, :, k : k + 1, :]
                    if k < 3:
                        Q[b, :, row, :] = ST[src, :, 4 + k : 5 + k, :]
                    if k < 2:
                        for s in range(S):
                            U[b, s, :, row, :] = ST[src, :, 7 + 2 * s + k : 8 + 2 * s + k, :]

        lane_own = MID + B * core + b
        cr = CR[...]

        def pick(l):
            return jnp.sum(jnp.where(l8 == l, cr, 0.0), axis=1, keepdims=True)

        c_own = pick(lane_own)
        c_side = [pick(lane_own + i[5]) for i in info]
        lo = jnp.where(info[0][0], -4, 0)
        hi = jnp.where(info[1][0], n + 3, n - 1)
        w_in, w_edge, corr, alive, linked = [], [], [], [], []
        for i in range(NI):
            r = NI * s8 + (i - 4)
            inside = (r >= lo) & (r <= hi)
            wall = ((r == 0) & (lo == 0)) | ((r == n - 1) & (hi == n - 1))
            links = jnp.where(wall, 1.0, 2.0)
            w_in.append(jnp.where(inside, 0.8 / (2.5 + links), 0.0))
            w_edge.append(jnp.where(inside, 0.8 / (1.5 + links), 0.0))
            c = jnp.where(r < 0, c_side[0], jnp.where(r >= n, c_side[1], c_own))
            corr.append(jnp.where(inside, c, 0.0))
            alive.append((r >= 0) & (r < n))
            linked.append(jnp.logical_not(((r == -1) & (lo == 0)) | ((r == n - 1) & (hi == n - 1))))

        def weight(i, j):
            if j == 0:
                return jnp.where(first, w_edge[i], w_in[i])
            if j == NT - 1:
                return jnp.where(last, w_edge[i], w_in[i])
            return w_in[i]

        def smooth(load, store):
            prv, cur = None, [load(i, 0) for i in range(NI)]
            for j in range(NT):
                nxt = [load(i, j + 1) for i in range(NI)] if j < NT - 1 else None
                u, d, lf, rt = up(cur), down(cur), left_of(cur, prv), right_of(cur, nxt)
                for i in range(NI):
                    q = Q[b, j, at(i), :]
                    store(i, j, 0.2 * cur[i] + weight(i, j) * (q + ((u[i] + d[i]) + (lf[i] + rt[i]))))
                prv, cur = cur, nxt

        def put_v(i, j, x):
            MIDS[i, j] = x + corr[i]

        def put_phi(i, j, x):
            DV[i, j] = x

        smooth(lambda i, j: G[b, j, at(i), :], put_v)
        smooth(lambda i, j: MIDS[i, j], put_phi)
        cur = [DV[i, 0] for i in range(NI)]
        for j in range(NT):
            nxt = [DV[i, j + 1] for i in range(NI)] if j < NT - 1 else None
            u, rt = up(cur), right_of(cur, nxt)
            for i in range(NI):
                G[b, j, at(i), :] = jnp.where(alive[i], cur[i], 0.0)
                DV[i, j] = u[i] - cur[i]
                DH[i, j] = rt[i] - cur[i]
            cur = nxt

        def species(s, _):
            half_z = jnp.where(s == 0, 0.5, jnp.where(s == 2, 1.0, -0.5)).astype(F32)
            k1 = 0.1 * diff_s[s]

            def stage(load, store):
                prv, cur = None, [load(i, 0) for i in range(NI)]
                for j in range(NT):
                    nxt = [load(i, j + 1) for i in range(NI)] if j < NT - 1 else None
                    u, rt = up(cur), right_of(cur, nxt)
                    fv, fh = [], []
                    for i in range(NI):
                        f = (u[i] - cur[i]) + (u[i] + cur[i]) * (half_z * DV[i, j])
                        fv.append(jnp.where(linked[i], f, 0.0))
                        f = (rt[i] - cur[i]) + (rt[i] + cur[i]) * (half_z * DH[i, j])
                        fh.append(jnp.where(last, 0.0, f) if j == NT - 1 else f)
                    fd, fl = down(fv), left_of(fh, prv)
                    for i in range(NI):
                        store(i, j, cur[i], (fv[i] - fd[i]) + (fh[i] - fl[i]))
                    prv, cur = fh, nxt

            def put_mid(i, j, u, rate):
                MIDS[i, j] = u + k1 * rate

            def put_end(i, j, mid, rate):
                u = U[b, s, j, at(i), :]
                x = 0.5 * u + 0.5 * (mid + k1 * rate)
                U[b, s, j, at(i), :] = jnp.where(alive[i], x, 0.0)

            stage(lambda i, j: U[b, s, j, at(i), :], put_mid)
            stage(lambda i, j: MIDS[i, j], put_end)
            return 0

        lax.fori_loop(0, S, species, 0)
        for c in results(b):
            c.start()
        return 0

    lax.fori_loop(0, B, block, 0)
    for b in range(B):
        for c in results(b):
            c.wait()


ANY = pl.BlockSpec(memory_space=pl.ANY)
HBM = pl.BlockSpec(memory_space=pltpu.HBM)
VMEM = pl.BlockSpec(memory_space=pltpu.VMEM)
def limit(mib):
    return pltpu.CompilerParams(vmem_limit_bytes=mib * 1024 * 1024)


def tables(devices):
    return pltpu.SMEM((B,), jnp.int32), pltpu.SMEM((devices * B,), jnp.int32), pltpu.SMEM((B, 2, 3), jnp.int32)


def shaped(*shape):
    return jax.ShapeDtypeStruct(shape, F32)


def body(concentration, potential_guess, diffusivity, block_rows, block_home, face_match):
    devices = lax.axis_size(AXIS)
    concentration, potential_guess, block_rows, block_home, face_match, diffusivity = (
        pltpu.with_memory_space_constraint(x, pltpu.HBM)
        for x in (concentration, potential_guess, block_rows, block_home, face_match, diffusivity)
    )

    def swap(x, pairs):
        return lax.ppermute(x, AXIS, pairs)

    on_chip = [(i, i ^ 1) for i in range(devices)]
    off_chip = [(i, (i + 1 if i % 2 else i - 1) % devices) for i in range(devices)]
    def beyond(k):
        return [((i + k if i % 2 else i - k) % devices, i) for i in range(devices)]


    strips, msg_e, msg_o = pl.pallas_call(
        functools.partial(pack_kernel, devices),
        out_shape=(shaped(2 * B, NT, 16, 128), shaped(NT + 1, 16, 128), shaped(NT + 1, 16, 128)),
        in_specs=[HBM] * 5,
        out_specs=(VMEM, VMEM, VMEM),
        scratch_shapes=[
            pltpu.VMEM((B, S, NT, H, 128), F32),
            pltpu.VMEM((B, NT, H, 128), F32),
            pltpu.VMEM((B, NT, H, 128), F32),
            *tables(devices),
            pltpu.SemaphoreType.DMA((B,)),
            pltpu.SemaphoreType.DMA((3,)),
        ],
        compiler_params=limit(40),
        name="pack",
    )(concentration, potential_guess, block_rows, block_home, face_match)

    got_e = swap(msg_e, on_chip)
    core = lax.axis_index(AXIS) % 2
    chip = msg_o[NT, 0:8] + got_e[NT, 0:8]
    third = swap(chip, beyond(6))
    second = swap(chip, beyond(4))
    got_o = swap(msg_o.at[NT, 0:8].set(chip), off_chip)
    w2 = (
        chip
        + turn(got_o[NT, 0:8], 6, core)
        + turn(second, 12, core)
        + turn(third, 18, core)
    )
    w_other = swap(w2, on_chip)

    return pl.pallas_call(
        functools.partial(main_kernel, devices),
        out_shape=(shaped(B, S, ROWS, FACE), shaped(B, ROWS, FACE)),
        in_specs=[HBM] * 2 + [ANY] * 3 + [VMEM, VMEM] + [HBM] * 4,
        out_specs=(HBM, HBM),
        scratch_shapes=[
            pltpu.VMEM((B, S, NT, H, 128), F32),
            pltpu.VMEM((B, NT, H, 128), F32),
            pltpu.VMEM((B, NT, H, 128), F32),
            pltpu.VMEM((8, NT, 16, 128), F32),
            pltpu.VMEM((NI, NT, 8, 128), F32),
            pltpu.VMEM((NI, NT, 8, 128), F32),
            pltpu.VMEM((NI, NT, 8, 128), F32),
            pltpu.VMEM((8, 128), F32),
            *tables(devices),
            pltpu.SMEM((4,), F32),
            pltpu.SemaphoreType.DMA((B,)),
            pltpu.SemaphoreType.DMA((3,)),
            pltpu.SemaphoreType.DMA((B,)),
            pltpu.SemaphoreType.DMA((4,)),
        ],
        compiler_params=limit(40),
        name="transport",
    )(
        concentration, potential_guess, strips, got_e, got_o, w2, w_other,
        block_rows, block_home, face_match, diffusivity,
    )


def solution(mesh):
    in_specs = (
        P("blk", None, None, None),
        P("blk", None, None),
        P(),
        P("blk"),
        P(),
        P("blk", None, None),
    )
    out_specs = (P("blk", None, None, None), P("blk", None, None))
    return jax.shard_map(body, mesh=mesh, in_specs=in_specs, out_specs=out_specs, check_vma=False)
```

```python
import functools

import jax
import jax.numpy as jnp
from jax import lax
from jax.experimental import pallas as pl
from jax.experimental.pallas import tpu as pltpu
from jax.sharding import PartitionSpec as P

AXIS = "blk"
B, S, ROWS, FACE = 3, 4, 40, 1024
NT = FACE // 128
LO = 8
H = 56
NI = 6
VALENCES = (1.0, -1.0, 2.0, -1.0)
FAR = 152
W_IN, W_EDGE = 0.8 / 4.5, 0.8 / 3.5
WALL = -1000.0
MID = 18
F32 = jnp.float32


def face_info(match_s, home_s, b, side, me, devices):
    g = match_s[b, side, 0]
    pos = home_s[jnp.maximum(g, 0)]
    dev = lax.div(pos, jnp.int32(B))
    pb = pos - dev * B
    off = lax.rem(dev - me + 1 + devices, devices)
    return g >= 0, off, pb, match_s[b, side, 1], match_s[b, side, 2], (off - 1) * B + pb - b


def iota(shape, dim):
    return lax.broadcasted_iota(jnp.int32, shape, dim)


def pack_kernel(
    devices, conc, pot, rows, home, match, msg_e, msg_o, X, rows_s, home_s, match_s, sem, tab_sem,
):
    me = lax.axis_index(AXIS)
    core = lax.rem(me, 2)
    U, G, Q = planes_of(X)

    def copies(b):
        out = []
        for j in range(NT):
            cols = pl.ds(128 * j, 128)
            out.append(pltpu.make_async_copy(conc.at[b, :, :, cols], X.at[b, pl.ds(0, S), j, pl.ds(LO, ROWS), :], sem.at[b]))
            out.append(pltpu.make_async_copy(pot.at[b, :, cols], X.at[b, 4, j, pl.ds(LO, ROWS), :], sem.at[b]))
        return out

    tables = [
        pltpu.make_async_copy(src, dst, tab_sem.at[k])
        for k, (src, dst) in enumerate(((rows, rows_s), (home, home_s), (match, match_s)))
    ]
    for c in tables:
        c.start()
    for b in range(B):
        for c in copies(b):
            c.start()
    for c in tables:
        c.wait()

    rowid = iota((ROWS, 128), 0)
    lane = iota((ROWS, 128), 1)
    first, last = lane == 0, lane == 127
    zero = jnp.zeros((ROWS, 128), F32)
    l8, s8 = iota((8, 128), 1), iota((8, 128), 0)
    mirror = 127 - l8

    def block(b, carry):
        W, fe, fo = carry
        for c in copies(b):
            c.wait()
        n = rows_s[b]
        info = [face_info(match_s, home_s, b, side, me, devices) for side in range(2)]
        live = rowid < n
        pad = jnp.zeros((8, 128), F32)
        for j in range(NT):
            c = [U[b, s, j, LO : LO + ROWS, :] for s in range(S)]
            q = c[0] - c[1] + 2.0 * c[2] - c[3]
            Q[b, j, LO : LO + ROWS, :] = jnp.where(live, q, 0.0)
            G[b, j, LO : LO + ROWS, :] = jnp.where(live, G[b, j, LO : LO + ROWS, :], 0.0)
            G[b, j, 0:LO, :] = pad
            G[b, j, LO + ROWS : H, :] = pad
        op = [i[0].astype(F32) for i in info]
        links = (
            2.0
            - jnp.where(rowid == 0, 1.0 - op[0], 0.0)
            - jnp.where(rowid == n - 1, 1.0 - op[1], 0.0)
        )
        w_in = jnp.where(live, 0.8 / (2.5 + links), 0.0)
        w_edge = jnp.where(live, 0.8 / (1.5 + links), 0.0)
        g = [G[b, j, LO : LO + ROWS, :] for j in range(NT)]
        gr = [pltpu.roll(x, 1, 1) for x in g]
        gl = [pltpu.roll(x, 127, 1) for x in g]
        total = s_sum = t_sum = zero
        for j in range(NT):
            left = jnp.where(first, gr[j - 1] if j else zero, gr[j])
            right = jnp.where(last, gl[j + 1] if j < NT - 1 else zero, gl[j])
            near = (
                G[b, j, LO + 1 : LO + 1 + ROWS, :] + G[b, j, LO - 1 : LO - 1 + ROWS, :] + left + right
            )
            w, wf = w_in, W_IN
            if j in (0, NT - 1):
                edge = first if j == 0 else last
                w, wf = jnp.where(edge, w_edge, w_in), jnp.where(edge, W_EDGE, W_IN)
            q = Q[b, j, LO : LO + ROWS, :]
            sm = 0.2 * g[j] + w * (q + near)
            total += q - 0.5 * sm
            s_sum += sm
            t_sum += wf * g[j]
        own = t_sum - s_sum
        away = s_sum - 1.5 * t_sum
        ends = [rowid == 0, rowid == n - 1]
        total += jnp.where(ends[0], op[0] * own, 0.0) + jnp.where(ends[1], op[1] * own, 0.0)
        vals = [jnp.sum(total, keepdims=True)]
        vals.append(1.0 / jnp.full((1, 1), 512.0 * n.astype(F32) + 1024.0 * (op[0] + op[1]), F32))
        vals += [jnp.sum(jnp.where(e, away, 0.0), keepdims=True) for e in ends]
        vals += [
            jnp.full((1, 1), jnp.where(i[0], i[5].astype(F32), WALL), F32) for i in info
        ]
        col = jnp.zeros((8, 128), F32)
        for k, v in enumerate(vals):
            col = jnp.where(s8 == k, v, col)
        W = jnp.where(l8 == MID + B * core + b, col, W)
        for side in range(2):
            f = 2 * b + side
            is_open, off, _, _, rev, _ = info[side]
            even = is_open & (off == 2 - 2 * core)
            odd = is_open & (off == 2 * core)
            fe, fo = jnp.where(even, f, fe), jnp.where(odd, f, fo)
            strip = X.at[b, 6 + side]
            for k in range(4):
                row = LO + k if side == 0 else LO + n - 1 - k
                at = pl.ds(row, 1)
                strip[:, k : k + 1, :] = G[b, :, at, :]
                if k < 3:
                    strip[:, 4 + k : 5 + k, :] = Q[b, :, at, :]
                if k < 2:
                    for s in range(S):
                        strip[:, 7 + 2 * s + k : 8 + 2 * s + k, :] = U[b, s, :, at, :]
            strip[:, 15:16, :] = jnp.zeros((NT, 1, 128), F32)

            @pl.when(rev == 1)
            def _():
                for j in range(NT // 2):
                    for h in range(0, 16, 8):
                        x = strip[j, h : h + 8, :]
                        y = strip[NT - 1 - j, h : h + 8, :]
                        strip[j, h : h + 8, :] = jnp.take_along_axis(y, mirror, axis=1)
                        strip[NT - 1 - j, h : h + 8, :] = jnp.take_along_axis(x, mirror, axis=1)

        return W, fe, fo

    W, fe, fo = lax.fori_loop(
        0, B, block, (jnp.zeros((8, 128), F32), jnp.int32(0), jnp.int32(0))
    )
    for msg, f in ((msg_e, fe), (msg_o, fo)):
        for j in range(NT):
            msg[j] = X[f // 2, 6 + f % 2, j, 0:16, :]
        msg[NT, 0:8, :] = W
        msg[NT, 8:16, :] = jnp.zeros((8, 128), F32)


def planes_of(X):
    return X, X.at[:, 4], X.at[:, 5]


def chip_kernel(msg_o, got_e, chip):
    chip[0:8, :] = msg_o[NT, 0:8, :] + got_e[NT, 0:8, :]
    chip[8:, :] = jnp.zeros((FAR - 8, 128), F32)


def stamp_kernel(_, chip, msg_o):
    msg_o[NT, 0:8, :] = chip[0:8, :]


def join_kernel(chip, second, third, got_o, out):
    core = lax.rem(lax.axis_index(AXIS), 2)
    total = chip[0:8, :]
    for k, x in enumerate((got_o[NT, 0:8, :], second[0:8, :], third[0:8, :])):
        shift = 6 * (k + 1)
        total += jnp.where(core == 1, pltpu.roll(x, shift, 1), pltpu.roll(x, 128 - shift, 1))
    out[...] = total


def coarse(W):
    n = 48
    I, J = iota((n, 128), 0).astype(F32), iota((n, 128), 1).astype(F32)
    lane = J[0:1]
    Wt = jnp.transpose(jnp.concatenate([W, jnp.zeros((120, 128), F32)], axis=0))[0:n]
    row = [W[k : k + 1] for k in range(6)]
    col = [Wt[:, k : k + 1] for k in range(6)]
    to = [(col[4 + s] + I) == J for s in range(2)]
    fro = [(row[4 + s] + lane) == I for s in range(2)]
    r_row = row[0] + jnp.sum(
        jnp.where(to[0], col[2], 0.0) + jnp.where(to[1], col[3], 0.0), axis=0, keepdims=True
    )
    r_col = col[0] + jnp.sum(
        jnp.where(fro[0], row[2], 0.0) + jnp.where(fro[1], row[3], 0.0), axis=1, keepdims=True
    )
    links = to[0].astype(F32) + to[1].astype(F32)
    diag = jnp.where(I == J, 0.2, 0.0)
    g_row, g_col = 0.8 * r_row * row[1], 0.8 * r_col * col[1]
    m_row = links * (819.2 * row[1]) + diag
    m_col = links * (819.2 * col[1]) + diag
    x = g_col
    x = g_row + jnp.sum(m_row * x, axis=0, keepdims=True)
    x = g_col + jnp.sum(m_col * x, axis=1, keepdims=True)
    return g_row + jnp.sum(m_row * x, axis=0, keepdims=True)


def insert(U, G, Q, b, side, n, strip):
    for k in range(4):
        row = pl.ds(LO - 1 - k if side == 0 else LO + n + k, 1)
        G[b, :, row, :] = strip[0:NT, k : k + 1, :]
        if k < 3:
            Q[b, :, row, :] = strip[0:NT, 4 + k : 5 + k, :]
        if k < 2:
            for s in range(S):
                U[b, s, :, row, :] = strip[0:NT, 7 + 2 * s + k : 8 + 2 * s + k, :]


def prep_kernel(devices, _, got_e, rows, home, match, X, rows_s, home_s, match_s, tab_sem):
    me = lax.axis_index(AXIS)
    core = lax.rem(me, 2)
    U, G, Q = planes_of(X)
    pairs = ((rows, rows_s), (home, home_s), (match, match_s))
    loads = [pltpu.make_async_copy(src, dst, tab_sem.at[k]) for k, (src, dst) in enumerate(pairs)]
    for c in loads:
        c.start()
    for c in loads:
        c.wait()
    rowid = iota((ROWS, 128), 0)
    zero = jnp.zeros((8, 128), F32)

    def block(b, _):
        n = rows_s[b]
        live = rowid < n
        for j in range(NT):
            for s in range(S):
                U[b, s, j, LO : LO + ROWS, :] = jnp.where(live, U[b, s, j, LO : LO + ROWS, :], 0.0)
                U[b, s, j, 0:LO, :] = zero
                U[b, s, j, LO + ROWS : H, :] = zero
            Q[b, j, 0:LO, :] = zero
            Q[b, j, LO + ROWS : H, :] = zero
        for side in range(2):
            is_open, off, pb, pf, _, _ = face_info(match_s, home_s, b, side, me, devices)

            @pl.when(is_open & (off == 1))
            def _():
                insert(U, G, Q, b, side, n, X.at[pb, 6 + pf])

            @pl.when(is_open & (off == 2 - 2 * core))
            def _():
                insert(U, G, Q, b, side, n, got_e)

        return 0

    lax.fori_loop(0, B, block, 0)


def main_kernel(
    devices, _, w_mine, w_theirs, got_o, rows, home, match, diff,
    end_out, pot_out, X, LV, LH, MIDS, CR, rows_s, home_s, match_s, diff_s, out_sem, tab_sem,
):
    me = lax.axis_index(AXIS)
    core = lax.rem(me, 2)
    U, G, Q = planes_of(X)

    def end_copies(b, s):
        return [
            pltpu.make_async_copy(
                X.at[b, s, j, pl.ds(LO, ROWS), :], end_out.at[b, s, :, pl.ds(128 * j, 128)], out_sem.at[b]
            )
            for j in range(NT)
        ]

    def pot_copies(b):
        return [
            pltpu.make_async_copy(
                X.at[b, 4, j, pl.ds(LO, ROWS), :], pot_out.at[b, :, pl.ds(128 * j, 128)], out_sem.at[b]
            )
            for j in range(NT)
        ]

    pairs = ((rows, rows_s), (home, home_s), (match, match_s), (diff, diff_s))
    loads = [pltpu.make_async_copy(src, dst, tab_sem.at[k]) for k, (src, dst) in enumerate(pairs)]
    for c in loads:
        c.start()

    l8, s8 = iota((8, 128), 1), iota((8, 128), 0)
    in_chip = (l8 >= MID) & (l8 < MID + 6)
    W = w_mine[...] + jnp.where(in_chip, 0.0, w_theirs[...])
    CR[...] = jnp.broadcast_to(coarse(W), (8, 128))
    for c in loads:
        c.wait()

    first, last = l8 == 0, l8 == 127
    zero = jnp.zeros((8, 128), F32)

    def at(i):
        return pl.ds(4 + i, 8, stride=NI)

    def up(x):
        return x[1:] + [pltpu.roll(x[0], 7, 0)]

    def down(x):
        return [pltpu.roll(x[NI - 1], 1, 0)] + x[:-1]

    def right_of(x, nxt):
        return [
            jnp.where(last, zero if nxt is None else pltpu.roll(nxt[i], 127, 1), pltpu.roll(x[i], 127, 1))
            for i in range(NI)
        ]

    def left_of(x, prv):
        return [
            jnp.where(first, zero if prv is None else pltpu.roll(prv[i], 1, 1), pltpu.roll(x[i], 1, 1))
            for i in range(NI)
        ]

    def block(b, _):
        n = rows_s[b]
        info = [face_info(match_s, home_s, b, side, me, devices) for side in range(2)]
        for side in range(2):

            @pl.when(info[side][0] & (info[side][1] == 2 * core))
            def _():
                insert(U, G, Q, b, side, n, got_o)

        lane_own = MID + B * core + b
        cr = CR[...]

        def pick(l):
            return jnp.sum(jnp.where(l8 == l, cr, 0.0), axis=1, keepdims=True)

        c_own = pick(lane_own)
        c_side = [pick(lane_own + i[5]) for i in info]
        lo = jnp.where(info[0][0], -4, 0)
        hi = jnp.where(info[1][0], n + 3, n - 1)
        w_in, w_edge, corr, alive, linked = [], [], [], [], []
        for i in range(NI):
            r = NI * s8 + (i - 4)
            inside = (r >= lo) & (r <= hi)
            wall = ((r == 0) & (lo == 0)) | ((r == n - 1) & (hi == n - 1))
            links = jnp.where(wall, 1.0, 2.0)
            w_in.append(jnp.where(inside, 0.8 / (2.5 + links), 0.0))
            w_edge.append(jnp.where(inside, 0.8 / (1.5 + links), 0.0))
            c = jnp.where(r < 0, c_side[0], jnp.where(r >= n, c_side[1], c_own))
            corr.append(jnp.where(inside, c, 0.0))
            alive.append((r >= 0) & (r < n))
            linked.append(jnp.where(((r == -1) & (lo == 0)) | ((r == n - 1) & (hi == n - 1)), 0.0, 1.0))

        def weight(i, j):
            if j == 0:
                return jnp.where(first, w_edge[i], w_in[i])
            if j == NT - 1:
                return jnp.where(last, w_edge[i], w_in[i])
            return w_in[i]

        def smooth(load, store):
            prv, cur = None, [load(i, 0) for i in range(NI)]
            for j in range(NT):
                nxt = [load(i, j + 1) for i in range(NI)] if j < NT - 1 else None
                u, d, lf, rt = up(cur), down(cur), left_of(cur, prv), right_of(cur, nxt)
                for i in range(NI):
                    q = Q[b, j, at(i), :]
                    store(i, j, 0.2 * cur[i] + weight(i, j) * (q + ((u[i] + d[i]) + (lf[i] + rt[i]))))
                prv, cur = cur, nxt

        def put_v(i, j, x):
            MIDS[i, j] = x + corr[i]

        def put_phi(i, j, x):
            G[b, j, at(i), :] = jnp.where(alive[i], x, 0.0)
            LV[0, i, j] = x

        smooth(lambda i, j: G[b, j, at(i), :], put_v)
        smooth(lambda i, j: MIDS[i, j], put_phi)
        for c in pot_copies(b):
            c.start()

        def factors(ref, i, j, mask, step):
            half = step * (0.5 * mask)
            a, d = mask + half, mask - half
            ref[0, i, j], ref[1, i, j] = a, d
            ref[2, i, j], ref[3, i, j] = a + half, d - half

        one = jnp.ones((8, 128), F32)
        wall_right = jnp.where(last, 0.0, one)
        cur = [LV[0, i, 0] for i in range(NI)]
        for j in range(NT):
            nxt = [LV[0, i, j + 1] for i in range(NI)] if j < NT - 1 else None
            u, rt = up(cur), right_of(cur, nxt)
            for i in range(NI):
                factors(LV, i, j, linked[i], u[i] - cur[i])
                factors(LH, i, j, wall_right if j == NT - 1 else one, rt[i] - cur[i])
            cur = nxt

        def species(s, _):
            ia = jnp.where(s == 0, 0, jnp.where(s == 2, 2, 1))
            ib = jnp.where(s == 0, 1, jnp.where(s == 2, 3, 0))
            k1 = 0.1 * diff_s[s]
            k2 = 0.05 * diff_s[s]

            def stage(load, store):
                prv, cur = None, [load(i, 0) for i in range(NI)]
                for j in range(NT):
                    nxt = [load(i, j + 1) for i in range(NI)] if j < NT - 1 else None
                    u, rt = up(cur), right_of(cur, nxt)
                    fv = [u[i] * LV[ia, i, j] - cur[i] * LV[ib, i, j] for i in range(NI)]
                    fh = [rt[i] * LH[ia, i, j] - cur[i] * LH[ib, i, j] for i in range(NI)]
                    fd, fl = down(fv), left_of(fh, prv)
                    for i in range(NI):
                        store(i, j, cur[i], (fv[i] - fd[i]) + (fh[i] - fl[i]))
                    prv, cur = fh, nxt

            def put_mid(i, j, u, rate):
                MIDS[i, j] = u + k1 * rate

            def put_end(i, j, mid, rate):
                x = 0.5 * (U[b, s, j, at(i), :] + mid) + k2 * rate
                U[b, s, j, at(i), :] = jnp.where(alive[i], x, 0.0)

            stage(lambda i, j: U[b, s, j, at(i), :], put_mid)
            stage(lambda i, j: MIDS[i, j], put_end)
            for c in end_copies(b, s):
                c.start()
            return 0

        lax.fori_loop(0, S, species, 0)
        return 0

    lax.fori_loop(0, B, block, 0)
    for b in range(B):
        for c in pot_copies(b):
            c.wait()
        for s in range(S):
            for c in end_copies(b, s):
                c.wait()


HBM = pl.BlockSpec(memory_space=pltpu.HBM)
VMEM = pl.BlockSpec(memory_space=pltpu.VMEM)
def limit(mib):
    return pltpu.CompilerParams(vmem_limit_bytes=mib * 1024 * 1024)


def tables(devices):
    return pltpu.SMEM((B,), jnp.int32), pltpu.SMEM((devices * B,), jnp.int32), pltpu.SMEM((B, 2, 3), jnp.int32)


def shaped(*shape):
    return jax.ShapeDtypeStruct(shape, F32)


def body(concentration, potential_guess, diffusivity, block_rows, block_home, face_match):
    devices = lax.axis_size(AXIS)
    concentration, potential_guess, block_rows, block_home, face_match, diffusivity = (
        pltpu.with_memory_space_constraint(x, pltpu.HBM)
        for x in (concentration, potential_guess, block_rows, block_home, face_match, diffusivity)
    )

    def swap(x, pairs):
        return lax.ppermute(x, AXIS, pairs)

    on_chip = [(i, i ^ 1) for i in range(devices)]
    off_chip = [(i, (i + 1 if i % 2 else i - 1) % devices) for i in range(devices)]
    def beyond(k):
        return [((i + k if i % 2 else i - k) % devices, i) for i in range(devices)]


    state = pltpu.VMEM((B, S + 4, NT, H, 128), F32)
    message = pltpu.VMEM((NT + 1, 16, 128), F32)
    msg_e, msg_o, x = pl.pallas_call(
        functools.partial(pack_kernel, devices),
        out_shape=(message, message, state),
        in_specs=[HBM] * 5,
        out_specs=(VMEM,) * 3,
        scratch_shapes=[
            *tables(devices),
            pltpu.SemaphoreType.DMA((B,)),
            pltpu.SemaphoreType.DMA((3,)),
        ],
        compiler_params=limit(40),
        name="pack",
    )(concentration, potential_guess, block_rows, block_home, face_match)

    got_e = swap(msg_e, on_chip)
    record = pltpu.VMEM((FAR, 128), F32)
    chip = pl.pallas_call(
        chip_kernel,
        out_shape=record,
        in_specs=[VMEM, VMEM],
        out_specs=VMEM,
        compiler_params=limit(1),
        name="chip",
    )(msg_o, got_e)
    msg_o = pl.pallas_call(
        stamp_kernel,
        out_shape=message,
        in_specs=[VMEM, VMEM],
        out_specs=VMEM,
        input_output_aliases={0: 0},
        compiler_params=limit(1),
        name="stamp",
    )(msg_o, chip)
    third = swap(chip, beyond(6))
    second = swap(chip, beyond(4))
    x = pl.pallas_call(
        functools.partial(prep_kernel, devices),
        out_shape=state,
        in_specs=[VMEM] * 2 + [HBM] * 3,
        out_specs=VMEM,
        scratch_shapes=[*tables(devices), pltpu.SemaphoreType.DMA((3,))],
        input_output_aliases={0: 0},
        compiler_params=limit(40),
        name="prep",
    )(x, got_e, block_rows, block_home, face_match)
    got_o = swap(msg_o, off_chip)
    x, chip = lax.optimization_barrier((x, chip))
    w2 = pl.pallas_call(
        join_kernel,
        out_shape=pltpu.VMEM((8, 128), F32),
        in_specs=[VMEM] * 4,
        out_specs=VMEM,
        compiler_params=limit(1),
        name="join",
    )(chip, second, third, got_o)
    w_other = swap(w2, on_chip)

    link = pltpu.VMEM((4, NI, NT, 8, 128), F32)
    out = pl.pallas_call(
        functools.partial(main_kernel, devices),
        out_shape=(shaped(B, S, ROWS, FACE), shaped(B, ROWS, FACE), state),
        in_specs=[VMEM] * 4 + [HBM] * 4,
        out_specs=(HBM, HBM, VMEM),
        scratch_shapes=[
            link,
            link,
            pltpu.VMEM((NI, NT, 8, 128), F32),
            pltpu.VMEM((8, 128), F32),
            *tables(devices),
            pltpu.SMEM((4,), F32),
            pltpu.SemaphoreType.DMA((B,)),
            pltpu.SemaphoreType.DMA((4,)),
        ],
        input_output_aliases={0: 2},
        compiler_params=limit(40),
        name="transport",
    )(x, w2, w_other, got_o, block_rows, block_home, face_match, diffusivity)
    return out[0], out[1]


def solution(mesh):
    in_specs = (
        P("blk", None, None, None),
        P("blk", None, None),
        P(),
        P("blk"),
        P(),
        P("blk", None, None),
    )
    out_specs = (P("blk", None, None, None), P("blk", None, None))
    return jax.shard_map(body, mesh=mesh, in_specs=in_specs, out_specs=out_specs, check_vma=False)
```

```python
import functools

import jax
import jax.numpy as jnp
from jax import lax
from jax.experimental import pallas as pl
from jax.experimental.pallas import tpu as pltpu
from jax.sharding import PartitionSpec as P

AXIS = "blk"
B, S, ROWS, FACE = 3, 4, 40, 1024
NT = FACE // 128
LO = 8
H = 56
NI = 6
VALENCES = (1.0, -1.0, 2.0, -1.0)
GUESS, CHARGE, STRIP, LEFT, RIGHT, WIDE, PLANES = 4, 5, 6, 8, 12, 16, 17
FAR = 152
W_IN, W_EDGE = 0.8 / 4.5, 0.8 / 3.5
WALL = -1000.0
MID = 18
F32 = jnp.float32


def face_info(match_s, home_s, b, side, me, devices):
    g = match_s[b, side, 0]
    pos = home_s[jnp.maximum(g, 0)]
    dev = lax.div(pos, jnp.int32(B))
    pb = pos - dev * B
    off = lax.rem(dev - me + 1 + devices, devices)
    return g >= 0, off, pb, match_s[b, side, 1], match_s[b, side, 2], (off - 1) * B + pb - b


def iota(shape, dim):
    return lax.broadcasted_iota(jnp.int32, shape, dim)


def pack_kernel(
    devices, conc, pot, rows, home, match, msg_e, msg_o, X, rows_s, home_s, match_s, sem, tab_sem,
):
    me = lax.axis_index(AXIS)
    core = lax.rem(me, 2)
    U, G, Q = planes_of(X)

    def copies(b):
        out = []
        for j in range(NT):
            cols = pl.ds(128 * j, 128)
            out.append(pltpu.make_async_copy(conc.at[b, :, :, cols], X.at[b, pl.ds(0, S), j, pl.ds(LO, ROWS), :], sem.at[b]))
            out.append(pltpu.make_async_copy(pot.at[b, :, cols], X.at[b, 4, j, pl.ds(LO, ROWS), :], sem.at[b]))
        return out

    tables = [
        pltpu.make_async_copy(src, dst, tab_sem.at[k])
        for k, (src, dst) in enumerate(((rows, rows_s), (home, home_s), (match, match_s)))
    ]
    for c in tables:
        c.start()
    for b in range(B):
        for c in copies(b):
            c.start()
    for c in tables:
        c.wait()

    rowid = iota((ROWS, 128), 0)
    lane = iota((ROWS, 128), 1)
    first, last = lane == 0, lane == 127
    zero = jnp.zeros((ROWS, 128), F32)
    l8, s8 = iota((8, 128), 1), iota((8, 128), 0)
    mirror = 127 - l8

    def block(b, carry):
        W, fe, fo = carry
        for c in copies(b):
            c.wait()
        n = rows_s[b]
        info = [face_info(match_s, home_s, b, side, me, devices) for side in range(2)]
        live = rowid < n
        pad = jnp.zeros((8, 128), F32)
        for j in range(NT):
            c = [U[b, s, j, LO : LO + ROWS, :] for s in range(S)]
            q = c[0] - c[1] + 2.0 * c[2] - c[3]
            Q[b, j, LO : LO + ROWS, :] = jnp.where(live, q, 0.0)
            G[b, j, LO : LO + ROWS, :] = jnp.where(live, G[b, j, LO : LO + ROWS, :], 0.0)
            G[b, j, 0:LO, :] = pad
            G[b, j, LO + ROWS : H, :] = pad
        op = [i[0].astype(F32) for i in info]
        links = (
            2.0
            - jnp.where(rowid == 0, 1.0 - op[0], 0.0)
            - jnp.where(rowid == n - 1, 1.0 - op[1], 0.0)
        )
        w_in = jnp.where(live, 0.8 / (2.5 + links), 0.0)
        w_edge = jnp.where(live, 0.8 / (1.5 + links), 0.0)
        g = [G[b, j, LO : LO + ROWS, :] for j in range(NT)]
        gr = [pltpu.roll(x, 1, 1) for x in g]
        gl = [pltpu.roll(x, 127, 1) for x in g]
        total = s_sum = t_sum = zero
        for j in range(NT):
            left = jnp.where(first, gr[j - 1] if j else zero, gr[j])
            right = jnp.where(last, gl[j + 1] if j < NT - 1 else zero, gl[j])
            near = (
                G[b, j, LO + 1 : LO + 1 + ROWS, :] + G[b, j, LO - 1 : LO - 1 + ROWS, :] + left + right
            )
            w, wf = w_in, W_IN
            if j in (0, NT - 1):
                edge = first if j == 0 else last
                w, wf = jnp.where(edge, w_edge, w_in), jnp.where(edge, W_EDGE, W_IN)
            q = Q[b, j, LO : LO + ROWS, :]
            sm = 0.2 * g[j] + w * (q + near)
            total += q - 0.5 * sm
            s_sum += sm
            t_sum += wf * g[j]
        own = t_sum - s_sum
        away = s_sum - 1.5 * t_sum
        ends = [rowid == 0, rowid == n - 1]
        total += jnp.where(ends[0], op[0] * own, 0.0) + jnp.where(ends[1], op[1] * own, 0.0)
        vals = [jnp.sum(total, keepdims=True)]
        vals.append(1.0 / jnp.full((1, 1), 512.0 * n.astype(F32) + 1024.0 * (op[0] + op[1]), F32))
        vals += [jnp.sum(jnp.where(e, away, 0.0), keepdims=True) for e in ends]
        vals += [
            jnp.full((1, 1), jnp.where(i[0], i[5].astype(F32), WALL), F32) for i in info
        ]
        col = jnp.zeros((8, 128), F32)
        for k, v in enumerate(vals):
            col = jnp.where(s8 == k, v, col)
        W = jnp.where(l8 == MID + B * core + b, col, W)
        for side in range(2):
            f = 2 * b + side
            is_open, off, _, _, rev, _ = info[side]
            even = is_open & (off == 2 - 2 * core)
            odd = is_open & (off == 2 * core)
            fe, fo = jnp.where(even, f, fe), jnp.where(odd, f, fo)
            strip = X.at[b, 6 + side]
            for k in range(4):
                row = LO + k if side == 0 else LO + n - 1 - k
                at = pl.ds(row, 1)
                strip[:, k : k + 1, :] = G[b, :, at, :]
                if k < 3:
                    strip[:, 4 + k : 5 + k, :] = Q[b, :, at, :]
                if k < 2:
                    for s in range(S):
                        strip[:, 7 + 2 * s + k : 8 + 2 * s + k, :] = U[b, s, :, at, :]
            strip[:, 15:16, :] = jnp.zeros((NT, 1, 128), F32)

            @pl.when(rev == 1)
            def _():
                for j in range(NT // 2):
                    for h in range(0, 16, 8):
                        x = strip[j, h : h + 8, :]
                        y = strip[NT - 1 - j, h : h + 8, :]
                        strip[j, h : h + 8, :] = jnp.take_along_axis(y, mirror, axis=1)
                        strip[NT - 1 - j, h : h + 8, :] = jnp.take_along_axis(x, mirror, axis=1)

        return W, fe, fo

    W, fe, fo = lax.fori_loop(
        0, B, block, (jnp.zeros((8, 128), F32), jnp.int32(0), jnp.int32(0))
    )
    for msg, f in ((msg_e, fe), (msg_o, fo)):
        for j in range(NT):
            msg[j] = X[f // 2, 6 + f % 2, j, 0:16, :]
        msg[NT, 0:8, :] = W
        msg[NT, 8:16, :] = jnp.zeros((8, 128), F32)


def planes_of(X):
    return X, X.at[:, 4], X.at[:, 5]


def chip_kernel(msg_o, got_e, chip):
    chip[0:8, :] = msg_o[NT, 0:8, :] + got_e[NT, 0:8, :]
    chip[8:, :] = jnp.zeros((FAR - 8, 128), F32)


def stamp_kernel(_, chip, msg_o):
    msg_o[NT, 0:8, :] = chip[0:8, :]


def join_kernel(chip, second, third, got_o, out):
    core = lax.rem(lax.axis_index(AXIS), 2)
    total = chip[0:8, :]
    for k, x in enumerate((got_o[NT, 0:8, :], second[0:8, :], third[0:8, :])):
        shift = 6 * (k + 1)
        total += jnp.where(core == 1, pltpu.roll(x, shift, 1), pltpu.roll(x, 128 - shift, 1))
    out[...] = total


def coarse(W):
    n = 48
    I, J = iota((n, 128), 0).astype(F32), iota((n, 128), 1).astype(F32)
    lane = J[0:1]
    Wt = jnp.transpose(jnp.concatenate([W, jnp.zeros((120, 128), F32)], axis=0))[0:n]
    row = [W[k : k + 1] for k in range(6)]
    col = [Wt[:, k : k + 1] for k in range(6)]
    to = [(col[4 + s] + I) == J for s in range(2)]
    fro = [(row[4 + s] + lane) == I for s in range(2)]
    r_row = row[0] + jnp.sum(
        jnp.where(to[0], col[2], 0.0) + jnp.where(to[1], col[3], 0.0), axis=0, keepdims=True
    )
    r_col = col[0] + jnp.sum(
        jnp.where(fro[0], row[2], 0.0) + jnp.where(fro[1], row[3], 0.0), axis=1, keepdims=True
    )
    links = to[0].astype(F32) + to[1].astype(F32)
    diag = jnp.where(I == J, 0.2, 0.0)
    g_row, g_col = 0.8 * r_row * row[1], 0.8 * r_col * col[1]
    m_row = links * (819.2 * row[1]) + diag
    m_col = links * (819.2 * col[1]) + diag
    x = g_col
    x = g_row + jnp.sum(m_row * x, axis=0, keepdims=True)
    x = g_col + jnp.sum(m_col * x, axis=1, keepdims=True)
    return g_row + jnp.sum(m_row * x, axis=0, keepdims=True)


def shift_right(tiles, last):
    moved = [pltpu.roll(t, 127, 1) for t in tiles] + [jnp.zeros_like(tiles[0])]
    return [jnp.where(last, moved[j + 1], moved[j]) for j in range(NT)]


def shift_left(tiles, first):
    moved = [jnp.zeros_like(tiles[0])] + [pltpu.roll(t, 1, 1) for t in tiles]
    return [jnp.where(first, moved[j], moved[j + 1]) for j in range(NT)]


def insert(U, G, Q, b, side, n, strip):
    for k in range(4):
        row = pl.ds(LO - 1 - k if side == 0 else LO + n + k, 1)
        G[b, :, row, :] = strip[0:NT, k : k + 1, :]
        if k < 3:
            Q[b, :, row, :] = strip[0:NT, 4 + k : 5 + k, :]
        if k < 2:
            for s in range(S):
                U[b, s, :, row, :] = strip[0:NT, 7 + 2 * s + k : 8 + 2 * s + k, :]


def prep_kernel(devices, _, got_e, rows, home, match, X, rows_s, home_s, match_s, tab_sem):
    me = lax.axis_index(AXIS)
    core = lax.rem(me, 2)
    U, G, Q = planes_of(X)
    pairs = ((rows, rows_s), (home, home_s), (match, match_s))
    loads = [pltpu.make_async_copy(src, dst, tab_sem.at[k]) for k, (src, dst) in enumerate(pairs)]
    for c in loads:
        c.start()
    for c in loads:
        c.wait()
    rowid = iota((ROWS, 128), 0)
    zero = jnp.zeros((8, 128), F32)
    first, last = iota((8, 128), 1) == 0, iota((8, 128), 1) == 127

    def block(b, _):
        n = rows_s[b]
        live = rowid < n
        for j in range(NT):
            for s in range(S):
                U[b, s, j, LO : LO + ROWS, :] = jnp.where(live, U[b, s, j, LO : LO + ROWS, :], 0.0)
                U[b, s, j, 0:LO, :] = zero
                U[b, s, j, LO + ROWS : H, :] = zero
            Q[b, j, 0:LO, :] = zero
            Q[b, j, LO + ROWS : H, :] = zero
        for side in range(2):
            is_open, off, pb, pf, _, _ = face_info(match_s, home_s, b, side, me, devices)

            @pl.when(is_open & (off == 1))
            def _():
                insert(U, G, Q, b, side, n, X.at[pb, 6 + pf])

            @pl.when(is_open & (off == 2 - 2 * core))
            def _():
                insert(U, G, Q, b, side, n, got_e)

        for i in range(NI):
            at = pl.ds(4 + i, 8, stride=NI)
            g = [X[b, GUESS, j, at, :] for j in range(NT)]
            for j, (x, y) in enumerate(zip(shift_left(g, first), shift_right(g, last))):
                X[b, WIDE, j, at, :] = X[b, CHARGE, j, at, :] + (x + y)

        def species(s, _):
            for i in range(NI):
                at = pl.ds(4 + i, 8, stride=NI)
                u = [X[b, s, j, at, :] for j in range(NT)]
                for j, (x, y) in enumerate(zip(shift_left(u, first), shift_right(u, last))):
                    X[b, LEFT + s, j, at, :] = x
                    X[b, RIGHT + s, j, at, :] = y
            return 0

        lax.fori_loop(0, S, species, 0, unroll=True)
        return 0

    lax.fori_loop(0, B, block, 0)


def main_kernel(
    devices, _, w_mine, w_theirs, got_o, rows, home, match, diff,
    end_out, pot_out, X, LV, LH, MIDS, CR, SL, SR, rows_s, home_s, match_s, diff_s, out_sem, tab_sem,
):
    me = lax.axis_index(AXIS)
    core = lax.rem(me, 2)
    U, G, Q = planes_of(X)

    def end_copies(b, s):
        return [
            pltpu.make_async_copy(
                X.at[b, s, j, pl.ds(LO, ROWS), :], end_out.at[b, s, :, pl.ds(128 * j, 128)], out_sem.at[b]
            )
            for j in range(NT)
        ]

    def pot_copies(b):
        return [
            pltpu.make_async_copy(
                X.at[b, 4, j, pl.ds(LO, ROWS), :], pot_out.at[b, :, pl.ds(128 * j, 128)], out_sem.at[b]
            )
            for j in range(NT)
        ]

    pairs = ((rows, rows_s), (home, home_s), (match, match_s), (diff, diff_s))
    loads = [pltpu.make_async_copy(src, dst, tab_sem.at[k]) for k, (src, dst) in enumerate(pairs)]
    for c in loads:
        c.start()

    l8, s8 = iota((8, 128), 1), iota((8, 128), 0)
    in_chip = (l8 >= MID) & (l8 < MID + 6)
    W = w_mine[...] + jnp.where(in_chip, 0.0, w_theirs[...])
    CR[...] = jnp.broadcast_to(coarse(W), (8, 128))
    first, last = l8 == 0, l8 == 127
    for h in range(0, 16, 8):
        strip = [got_o[j, h : h + 8, :] for j in range(NT)]
        for j, (x, y) in enumerate(zip(shift_left(strip, first), shift_right(strip, last))):
            SL[j, h : h + 8, :] = x
            SR[j, h : h + 8, :] = y
    for c in loads:
        c.wait()

    zero = jnp.zeros((8, 128), F32)

    def at(i):
        return pl.ds(4 + i, 8, stride=NI)

    def up(x):
        return x[1:] + [pltpu.roll(x[0], 7, 0)]

    def down(x):
        return [pltpu.roll(x[NI - 1], 1, 0)] + x[:-1]

    def right_of(x, nxt):
        return [
            jnp.where(last, zero if nxt is None else pltpu.roll(nxt[i], 127, 1), pltpu.roll(x[i], 127, 1))
            for i in range(NI)
        ]

    def left_of(x, prv):
        return [
            jnp.where(first, zero if prv is None else pltpu.roll(prv[i], 1, 1), pltpu.roll(x[i], 1, 1))
            for i in range(NI)
        ]

    def block(b, _):
        n = rows_s[b]
        info = [face_info(match_s, home_s, b, side, me, devices) for side in range(2)]
        for side in range(2):

            @pl.when(info[side][0] & (info[side][1] == 2 * core))
            def _():
                insert(U, G, Q, b, side, n, got_o)
                for k in range(3):
                    row = pl.ds(LO - 1 - k if side == 0 else LO + n + k, 1)
                    sides = SL[:, k : k + 1, :] + SR[:, k : k + 1, :]
                    X[b, WIDE, :, row, :] = got_o[0:NT, 4 + k : 5 + k, :] + sides
                    if k < 2:
                        for s in range(S):
                            m = 7 + 2 * s + k
                            X[b, LEFT + s, :, row, :] = SL[:, m : m + 1, :]
                            X[b, RIGHT + s, :, row, :] = SR[:, m : m + 1, :]

        lane_own = MID + B * core + b
        cr = CR[...]

        def pick(l):
            return jnp.sum(jnp.where(l8 == l, cr, 0.0), axis=1, keepdims=True)

        c_own = pick(lane_own)
        c_side = [pick(lane_own + i[5]) for i in info]
        lo = jnp.where(info[0][0], -4, 0)
        hi = jnp.where(info[1][0], n + 3, n - 1)
        w_in, w_edge, corr, alive, linked = [], [], [], [], []
        for i in range(NI):
            r = NI * s8 + (i - 4)
            inside = (r >= lo) & (r <= hi)
            wall = ((r == 0) & (lo == 0)) | ((r == n - 1) & (hi == n - 1))
            links = jnp.where(wall, 1.0, 2.0)
            w_in.append(jnp.where(inside, 0.8 / (2.5 + links), 0.0))
            w_edge.append(jnp.where(inside, 0.8 / (1.5 + links), 0.0))
            c = jnp.where(r < 0, c_side[0], jnp.where(r >= n, c_side[1], c_own))
            corr.append(jnp.where(inside, c, 0.0))
            alive.append((r >= 0) & (r < n))
            linked.append(jnp.where(((r == -1) & (lo == 0)) | ((r == n - 1) & (hi == n - 1)), 0.0, 1.0))

        def weight(i, j):
            if j == 0:
                return jnp.where(first, w_edge[i], w_in[i])
            if j == NT - 1:
                return jnp.where(last, w_edge[i], w_in[i])
            return w_in[i]

        for j in range(NT):
            cur = [G[b, j, at(i), :] for i in range(NI)]
            u, d = up(cur), down(cur)
            for i in range(NI):
                x = 0.2 * cur[i] + weight(i, j) * (X[b, WIDE, j, at(i), :] + (u[i] + d[i]))
                MIDS[i, j] = x + corr[i]
        prv, cur = None, [MIDS[i, 0] for i in range(NI)]
        for j in range(NT):
            nxt = [MIDS[i, j + 1] for i in range(NI)] if j < NT - 1 else None
            u, d, lf, rt = up(cur), down(cur), left_of(cur, prv), right_of(cur, nxt)
            for i in range(NI):
                q = Q[b, j, at(i), :]
                x = 0.2 * cur[i] + weight(i, j) * (q + ((u[i] + d[i]) + (lf[i] + rt[i])))
                G[b, j, at(i), :] = jnp.where(alive[i], x, 0.0)
                LV[0, i, j] = x
            prv, cur = cur, nxt
        for c in pot_copies(b):
            c.start()

        one = jnp.ones((8, 128), F32)
        edge_right, edge_left = jnp.where(last, 0.0, one), jnp.where(first, 0.0, one)
        prv, cur = None, [LV[0, i, 0] for i in range(NI)]
        for j in range(NT):
            nxt = [LV[0, i, j + 1] for i in range(NI)] if j < NT - 1 else None
            u, rt = up(cur), right_of(cur, nxt)
            m = edge_right if j == NT - 1 else one
            ml = edge_left if j == 0 else one
            step = [(0.5 * m) * (rt[i] - cur[i]) for i in range(NI)]
            past = left_of(step, prv)
            for i in range(NI):
                half = (0.5 * linked[i]) * (u[i] - cur[i])
                a, d = linked[i] + half, linked[i] - half
                LV[0, i, j], LV[1, i, j], LV[2, i, j], LV[3, i, j] = a, d, a + half, d - half
                a, d, al, dl = m + step[i], m - step[i], ml + past[i], ml - past[i]
                LH[0, i, j], LH[1, i, j], LH[2, i, j] = a, dl, d + al
                LH[3, i, j], LH[4, i, j], LH[5, i, j] = d, al, a + dl
                LH[6, i, j], LH[7, i, j] = a + step[i], dl - past[i]
                LH[8, i, j] = (d - step[i]) + (al + past[i])
            prv, cur = step, nxt

        def species(s, _):
            ia = jnp.where(s == 0, 0, jnp.where(s == 2, 2, 1))
            ib = jnp.where(s == 0, 1, jnp.where(s == 2, 3, 0))
            k1 = 0.1 * diff_s[s]
            k2 = 0.05 * diff_s[s]

            ih = jnp.where(s == 0, 0, jnp.where(s == 2, 6, 3))

            def rates(j, cur, lf, rt):
                u = up(cur)
                fv = [u[i] * LV[ia, i, j] - cur[i] * LV[ib, i, j] for i in range(NI)]
                fd = down(fv)
                fh = [
                    (rt[i] * LH[ih, i, j] + lf[i] * LH[ih + 1, i, j]) - cur[i] * LH[ih + 2, i, j]
                    for i in range(NI)
                ]
                return [(fv[i] - fd[i]) + fh[i] for i in range(NI)]

            for j in range(NT):
                cur, lf, rt = ([X[b, p + s, j, at(i), :] for i in range(NI)] for p in (0, LEFT, RIGHT))
                rate = rates(j, cur, lf, rt)
                for i in range(NI):
                    MIDS[i, j] = cur[i] + k1 * rate[i]
            prv, cur = None, [MIDS[i, 0] for i in range(NI)]
            for j in range(NT):
                nxt = [MIDS[i, j + 1] for i in range(NI)] if j < NT - 1 else None
                rate = rates(j, cur, left_of(cur, prv), right_of(cur, nxt))
                for i in range(NI):
                    x = 0.5 * (U[b, s, j, at(i), :] + cur[i]) + k2 * rate[i]
                    U[b, s, j, at(i), :] = jnp.where(alive[i], x, 0.0)
                prv, cur = cur, nxt
            for c in end_copies(b, s):
                c.start()
            return 0

        lax.fori_loop(0, S, species, 0, unroll=True)
        return 0

    lax.fori_loop(0, B, block, 0)
    for b in range(B):
        for c in pot_copies(b):
            c.wait()
        for s in range(S):
            for c in end_copies(b, s):
                c.wait()


HBM = pl.BlockSpec(memory_space=pltpu.HBM)
VMEM = pl.BlockSpec(memory_space=pltpu.VMEM)
def limit(mib):
    return pltpu.CompilerParams(vmem_limit_bytes=mib * 1024 * 1024)


def tables(devices):
    return pltpu.SMEM((B,), jnp.int32), pltpu.SMEM((devices * B,), jnp.int32), pltpu.SMEM((B, 2, 3), jnp.int32)


def shaped(*shape):
    return jax.ShapeDtypeStruct(shape, F32)


def body(concentration, potential_guess, diffusivity, block_rows, block_home, face_match):
    devices = lax.axis_size(AXIS)
    concentration, potential_guess, block_rows, block_home, face_match, diffusivity = (
        pltpu.with_memory_space_constraint(x, pltpu.HBM)
        for x in (concentration, potential_guess, block_rows, block_home, face_match, diffusivity)
    )

    def swap(x, pairs):
        return lax.ppermute(x, AXIS, pairs)

    on_chip = [(i, i ^ 1) for i in range(devices)]
    off_chip = [(i, (i + 1 if i % 2 else i - 1) % devices) for i in range(devices)]
    def beyond(k):
        return [((i + k if i % 2 else i - k) % devices, i) for i in range(devices)]


    state = pltpu.VMEM((B, PLANES, NT, H, 128), F32)
    message = pltpu.VMEM((NT + 1, 16, 128), F32)
    msg_e, msg_o, x = pl.pallas_call(
        functools.partial(pack_kernel, devices),
        out_shape=(message, message, state),
        in_specs=[HBM] * 5,
        out_specs=(VMEM,) * 3,
        scratch_shapes=[
            *tables(devices),
            pltpu.SemaphoreType.DMA((B,)),
            pltpu.SemaphoreType.DMA((3,)),
        ],
        compiler_params=limit(40),
        name="pack",
    )(concentration, potential_guess, block_rows, block_home, face_match)

    got_e = swap(msg_e, on_chip)
    record = pltpu.VMEM((FAR, 128), F32)
    chip = pl.pallas_call(
        chip_kernel,
        out_shape=record,
        in_specs=[VMEM, VMEM],
        out_specs=VMEM,
        compiler_params=limit(1),
        name="chip",
    )(msg_o, got_e)
    msg_o = pl.pallas_call(
        stamp_kernel,
        out_shape=message,
        in_specs=[VMEM, VMEM],
        out_specs=VMEM,
        input_output_aliases={0: 0},
        compiler_params=limit(1),
        name="stamp",
    )(msg_o, chip)
    third = swap(chip, beyond(6))
    second = swap(chip, beyond(4))
    x = pl.pallas_call(
        functools.partial(prep_kernel, devices),
        out_shape=state,
        in_specs=[VMEM] * 2 + [HBM] * 3,
        out_specs=VMEM,
        scratch_shapes=[*tables(devices), pltpu.SemaphoreType.DMA((3,))],
        input_output_aliases={0: 0},
        compiler_params=limit(40),
        name="prep",
    )(x, got_e, block_rows, block_home, face_match)
    got_o = swap(msg_o, off_chip)
    x, chip = lax.optimization_barrier((x, chip))
    w2 = pl.pallas_call(
        join_kernel,
        out_shape=pltpu.VMEM((8, 128), F32),
        in_specs=[VMEM] * 4,
        out_specs=VMEM,
        compiler_params=limit(1),
        name="join",
    )(chip, second, third, got_o)
    w_other = swap(w2, on_chip)

    out = pl.pallas_call(
        functools.partial(main_kernel, devices),
        out_shape=(shaped(B, S, ROWS, FACE), shaped(B, ROWS, FACE), state),
        in_specs=[VMEM] * 4 + [HBM] * 4,
        out_specs=(HBM, HBM, VMEM),
        scratch_shapes=[
            pltpu.VMEM((4, NI, NT, 8, 128), F32),
            pltpu.VMEM((9, NI, NT, 8, 128), F32),
            pltpu.VMEM((NI, NT, 8, 128), F32),
            pltpu.VMEM((8, 128), F32),
            pltpu.VMEM((NT, 16, 128), F32),
            pltpu.VMEM((NT, 16, 128), F32),
            *tables(devices),
            pltpu.SMEM((4,), F32),
            pltpu.SemaphoreType.DMA((B,)),
            pltpu.SemaphoreType.DMA((4,)),
        ],
        input_output_aliases={0: 2},
        compiler_params=limit(40),
        name="transport",
    )(x, w2, w_other, got_o, block_rows, block_home, face_match, diffusivity)
    return out[0], out[1]


def solution(mesh):
    in_specs = (
        P("blk", None, None, None),
        P("blk", None, None),
        P(),
        P("blk"),
        P(),
        P("blk", None, None),
    )
    out_specs = (P("blk", None, None, None), P("blk", None, None))
    return jax.shard_map(body, mesh=mesh, in_specs=in_specs, out_specs=out_specs, check_vma=False)
```

```python
import functools

import jax
import jax.numpy as jnp
from jax import lax
from jax.experimental import pallas as pl
from jax.experimental.pallas import tpu as pltpu
from jax.sharding import PartitionSpec as P

AXIS = "blk"
B, S, ROWS, FACE = 3, 4, 40, 1024
NT = FACE // 128
LO = 8
H = 56
NI = 6
VALENCES = (1.0, -1.0, 2.0, -1.0)
GUESS, CHARGE, STRIP, LEFT, RIGHT, WIDE, PLANES = 4, 5, 6, 8, 12, 16, 17
FAR = 152
W_IN, W_EDGE = 0.8 / 4.5, 0.8 / 3.5
WALL = -1000.0
MID = 18
F32 = jnp.float32


def face_info(match_s, home_s, b, side, me, devices):
    g = match_s[b, side, 0]
    pos = home_s[jnp.maximum(g, 0)]
    dev = lax.div(pos, jnp.int32(B))
    pb = pos - dev * B
    off = lax.rem(dev - me + 1 + devices, devices)
    return g >= 0, off, pb, match_s[b, side, 1], match_s[b, side, 2], (off - 1) * B + pb - b


def iota(shape, dim):
    return lax.broadcasted_iota(jnp.int32, shape, dim)


def pack_kernel(
    devices, conc, pot, rows, home, match, msg_e, msg_o, X, rows_s, home_s, match_s, sem, tab_sem,
):
    me = lax.axis_index(AXIS)
    core = lax.rem(me, 2)
    U, G, Q = planes_of(X)

    def copies(b):
        out = []
        for j in range(NT):
            cols = pl.ds(128 * j, 128)
            out.append(pltpu.make_async_copy(conc.at[b, :, :, cols], X.at[b, pl.ds(0, S), j, pl.ds(LO, ROWS), :], sem.at[b]))
            out.append(pltpu.make_async_copy(pot.at[b, :, cols], X.at[b, 4, j, pl.ds(LO, ROWS), :], sem.at[b]))
        return out

    tables = [
        pltpu.make_async_copy(src, dst, tab_sem.at[k])
        for k, (src, dst) in enumerate(((rows, rows_s), (home, home_s), (match, match_s)))
    ]
    for c in tables:
        c.start()
    for b in range(B):
        for c in copies(b):
            c.start()
    for c in tables:
        c.wait()

    rowid = iota((ROWS, 128), 0)
    lane = iota((ROWS, 128), 1)
    first, last = lane == 0, lane == 127
    zero = jnp.zeros((ROWS, 128), F32)
    l8, s8 = iota((8, 128), 1), iota((8, 128), 0)
    mirror = 127 - l8

    def block(b, carry):
        W, fe, fo = carry
        for c in copies(b):
            c.wait()
        n = rows_s[b]
        info = [face_info(match_s, home_s, b, side, me, devices) for side in range(2)]
        live = rowid < n
        pad = jnp.zeros((8, 128), F32)
        for j in range(NT):
            c = [U[b, s, j, LO : LO + ROWS, :] for s in range(S)]
            q = c[0] - c[1] + 2.0 * c[2] - c[3]
            Q[b, j, LO : LO + ROWS, :] = jnp.where(live, q, 0.0)
            G[b, j, LO : LO + ROWS, :] = jnp.where(live, G[b, j, LO : LO + ROWS, :], 0.0)
            G[b, j, 0:LO, :] = pad
            G[b, j, LO + ROWS : H, :] = pad
        op = [i[0].astype(F32) for i in info]
        links = (
            2.0
            - jnp.where(rowid == 0, 1.0 - op[0], 0.0)
            - jnp.where(rowid == n - 1, 1.0 - op[1], 0.0)
        )
        w_in = jnp.where(live, 0.8 / (2.5 + links), 0.0)
        w_edge = jnp.where(live, 0.8 / (1.5 + links), 0.0)
        g = [G[b, j, LO : LO + ROWS, :] for j in range(NT)]
        gr = [pltpu.roll(x, 1, 1) for x in g]
        gl = [pltpu.roll(x, 127, 1) for x in g]
        total = s_sum = t_sum = zero
        for j in range(NT):
            left = jnp.where(first, gr[j - 1] if j else zero, gr[j])
            right = jnp.where(last, gl[j + 1] if j < NT - 1 else zero, gl[j])
            near = (
                G[b, j, LO + 1 : LO + 1 + ROWS, :] + G[b, j, LO - 1 : LO - 1 + ROWS, :] + left + right
            )
            w, wf = w_in, W_IN
            if j in (0, NT - 1):
                edge = first if j == 0 else last
                w, wf = jnp.where(edge, w_edge, w_in), jnp.where(edge, W_EDGE, W_IN)
            q = Q[b, j, LO : LO + ROWS, :]
            sm = 0.2 * g[j] + w * (q + near)
            total += q - 0.5 * sm
            s_sum += sm
            t_sum += wf * g[j]
        own = t_sum - s_sum
        away = s_sum - 1.5 * t_sum
        ends = [rowid == 0, rowid == n - 1]
        total += jnp.where(ends[0], op[0] * own, 0.0) + jnp.where(ends[1], op[1] * own, 0.0)
        vals = [jnp.sum(total, keepdims=True)]
        vals.append(1.0 / jnp.full((1, 1), 512.0 * n.astype(F32) + 1024.0 * (op[0] + op[1]), F32))
        vals += [jnp.sum(jnp.where(e, away, 0.0), keepdims=True) for e in ends]
        vals += [
            jnp.full((1, 1), jnp.where(i[0], i[5].astype(F32), WALL), F32) for i in info
        ]
        col = jnp.zeros((8, 128), F32)
        for k, v in enumerate(vals):
            col = jnp.where(s8 == k, v, col)
        W = jnp.where(l8 == MID + B * core + b, col, W)
        for side in range(2):
            f = 2 * b + side
            is_open, off, _, _, rev, _ = info[side]
            even = is_open & (off == 2 - 2 * core)
            odd = is_open & (off == 2 * core)
            fe, fo = jnp.where(even, f, fe), jnp.where(odd, f, fo)
            strip = X.at[b, 6 + side]
            for k in range(4):
                row = LO + k if side == 0 else LO + n - 1 - k
                at = pl.ds(row, 1)
                strip[:, k : k + 1, :] = G[b, :, at, :]
                if k < 3:
                    strip[:, 4 + k : 5 + k, :] = Q[b, :, at, :]
                if k < 2:
                    for s in range(S):
                        strip[:, 7 + 2 * s + k : 8 + 2 * s + k, :] = U[b, s, :, at, :]
            strip[:, 15:16, :] = jnp.zeros((NT, 1, 128), F32)

            @pl.when(rev == 1)
            def _():
                for j in range(NT // 2):
                    for h in range(0, 16, 8):
                        x = strip[j, h : h + 8, :]
                        y = strip[NT - 1 - j, h : h + 8, :]
                        strip[j, h : h + 8, :] = jnp.take_along_axis(y, mirror, axis=1)
                        strip[NT - 1 - j, h : h + 8, :] = jnp.take_along_axis(x, mirror, axis=1)

        return W, fe, fo

    W, fe, fo = lax.fori_loop(
        0, B, block, (jnp.zeros((8, 128), F32), jnp.int32(0), jnp.int32(0))
    )
    for msg, f in ((msg_e, fe), (msg_o, fo)):
        for j in range(NT):
            msg[j] = X[f // 2, 6 + f % 2, j, 0:16, :]
        msg[NT, 0:8, :] = W
        msg[NT, 8:16, :] = jnp.zeros((8, 128), F32)


def planes_of(X):
    return X, X.at[:, 4], X.at[:, 5]


def chip_kernel(msg_o, got_e, chip):
    chip[0:8, :] = msg_o[NT, 0:8, :] + got_e[NT, 0:8, :]
    chip[8:, :] = jnp.zeros((FAR - 8, 128), F32)


def stamp_kernel(_, chip, msg_o):
    msg_o[NT, 0:8, :] = chip[0:8, :]


def join_kernel(chip, third, second, got_o, out):
    core = lax.rem(lax.axis_index(AXIS), 2)
    total = chip[0:8, :]
    for k, x in enumerate((got_o[NT, 0:8, :], second[0:8, :], third[0:8, :])):
        shift = 6 * (k + 1)
        total += jnp.where(core == 1, pltpu.roll(x, shift, 1), pltpu.roll(x, 128 - shift, 1))
    out[...] = total


def coarse(W):
    n = 48
    I, J = iota((n, 128), 0).astype(F32), iota((n, 128), 1).astype(F32)
    lane = J[0:1]
    Wt = jnp.transpose(jnp.concatenate([W, jnp.zeros((120, 128), F32)], axis=0))[0:n]
    row = [W[k : k + 1] for k in range(6)]
    col = [Wt[:, k : k + 1] for k in range(6)]
    to = [(col[4 + s] + I) == J for s in range(2)]
    fro = [(row[4 + s] + lane) == I for s in range(2)]
    r_row = row[0] + jnp.sum(
        jnp.where(to[0], col[2], 0.0) + jnp.where(to[1], col[3], 0.0), axis=0, keepdims=True
    )
    r_col = col[0] + jnp.sum(
        jnp.where(fro[0], row[2], 0.0) + jnp.where(fro[1], row[3], 0.0), axis=1, keepdims=True
    )
    links = to[0].astype(F32) + to[1].astype(F32)
    diag = jnp.where(I == J, 0.2, 0.0)
    g_row, g_col = 0.8 * r_row * row[1], 0.8 * r_col * col[1]
    m_row = links * (819.2 * row[1]) + diag
    m_col = links * (819.2 * col[1]) + diag
    x = g_col
    x = g_row + jnp.sum(m_row * x, axis=0, keepdims=True)
    x = g_col + jnp.sum(m_col * x, axis=1, keepdims=True)
    return g_row + jnp.sum(m_row * x, axis=0, keepdims=True)


def shift_right(tiles, last):
    moved = [pltpu.roll(t, 127, 1) for t in tiles] + [jnp.zeros_like(tiles[0])]
    return [jnp.where(last, moved[j + 1], moved[j]) for j in range(NT)]


def shift_left(tiles, first):
    moved = [jnp.zeros_like(tiles[0])] + [pltpu.roll(t, 1, 1) for t in tiles]
    return [jnp.where(first, moved[j], moved[j + 1]) for j in range(NT)]


def insert(U, G, Q, b, side, n, strip):
    for k in range(4):
        row = pl.ds(LO - 1 - k if side == 0 else LO + n + k, 1)
        G[b, :, row, :] = strip[0:NT, k : k + 1, :]
        if k < 3:
            Q[b, :, row, :] = strip[0:NT, 4 + k : 5 + k, :]
        if k < 2:
            for s in range(S):
                U[b, s, :, row, :] = strip[0:NT, 7 + 2 * s + k : 8 + 2 * s + k, :]


def prep_kernel(devices, _, got_e, rows, home, match, X, rows_s, home_s, match_s, tab_sem):
    me = lax.axis_index(AXIS)
    core = lax.rem(me, 2)
    U, G, Q = planes_of(X)
    pairs = ((rows, rows_s), (home, home_s), (match, match_s))
    loads = [pltpu.make_async_copy(src, dst, tab_sem.at[k]) for k, (src, dst) in enumerate(pairs)]
    for c in loads:
        c.start()
    for c in loads:
        c.wait()
    rowid = iota((ROWS, 128), 0)
    zero = jnp.zeros((8, 128), F32)
    first, last = iota((8, 128), 1) == 0, iota((8, 128), 1) == 127

    def block(b, _):
        n = rows_s[b]
        live = rowid < n
        for j in range(NT):
            for s in range(S):
                U[b, s, j, LO : LO + ROWS, :] = jnp.where(live, U[b, s, j, LO : LO + ROWS, :], 0.0)
                U[b, s, j, 0:LO, :] = zero
                U[b, s, j, LO + ROWS : H, :] = zero
            Q[b, j, 0:LO, :] = zero
            Q[b, j, LO + ROWS : H, :] = zero
        for side in range(2):
            is_open, off, pb, pf, _, _ = face_info(match_s, home_s, b, side, me, devices)

            @pl.when(is_open & (off == 1))
            def _():
                insert(U, G, Q, b, side, n, X.at[pb, 6 + pf])

            @pl.when(is_open & (off == 2 - 2 * core))
            def _():
                insert(U, G, Q, b, side, n, got_e)

        for i in range(NI):
            at = pl.ds(4 + i, 8, stride=NI)
            g = [X[b, GUESS, j, at, :] for j in range(NT)]
            for j, (x, y) in enumerate(zip(shift_left(g, first), shift_right(g, last))):
                X[b, WIDE, j, at, :] = X[b, CHARGE, j, at, :] + (x + y)

        def species(s, _):
            for i in range(NI):
                at = pl.ds(4 + i, 8, stride=NI)
                u = [X[b, s, j, at, :] for j in range(NT)]
                for j, (x, y) in enumerate(zip(shift_left(u, first), shift_right(u, last))):
                    X[b, LEFT + s, j, at, :] = x
                    X[b, RIGHT + s, j, at, :] = y
            return 0

        lax.fori_loop(0, S, species, 0, unroll=True)
        return 0

    lax.fori_loop(0, B, block, 0)


def main_kernel(
    devices, _, w_mine, w_theirs, got_o, rows, home, match, diff,
    end_out, pot_out, X, LV, LH, MIDS, CR, SL, SR, rows_s, home_s, match_s, diff_s, out_sem, tab_sem,
):
    me = lax.axis_index(AXIS)
    core = lax.rem(me, 2)
    U, G, Q = planes_of(X)

    def end_copies(b, s):
        return [
            pltpu.make_async_copy(
                X.at[b, s, j, pl.ds(LO, ROWS), :], end_out.at[b, s, :, pl.ds(128 * j, 128)], out_sem.at[b]
            )
            for j in range(NT)
        ]

    def pot_copies(b):
        return [
            pltpu.make_async_copy(
                X.at[b, 4, j, pl.ds(LO, ROWS), :], pot_out.at[b, :, pl.ds(128 * j, 128)], out_sem.at[b]
            )
            for j in range(NT)
        ]

    pairs = ((rows, rows_s), (home, home_s), (match, match_s), (diff, diff_s))
    loads = [pltpu.make_async_copy(src, dst, tab_sem.at[k]) for k, (src, dst) in enumerate(pairs)]
    for c in loads:
        c.start()

    l8, s8 = iota((8, 128), 1), iota((8, 128), 0)
    in_chip = (l8 >= MID) & (l8 < MID + 6)
    W = w_mine[...] + jnp.where(in_chip, 0.0, w_theirs[...])
    CR[...] = jnp.broadcast_to(coarse(W), (8, 128))
    first, last = l8 == 0, l8 == 127
    for h in range(0, 16, 8):
        strip = [got_o[j, h : h + 8, :] for j in range(NT)]
        for j, (x, y) in enumerate(zip(shift_left(strip, first), shift_right(strip, last))):
            SL[j, h : h + 8, :] = x
            SR[j, h : h + 8, :] = y
    for c in loads:
        c.wait()

    zero = jnp.zeros((8, 128), F32)

    def at(i):
        return pl.ds(4 + i, 8, stride=NI)

    def up(x):
        return x[1:] + [pltpu.roll(x[0], 7, 0)]

    def down(x):
        return [pltpu.roll(x[NI - 1], 1, 0)] + x[:-1]

    def right_of(x, nxt):
        return [
            jnp.where(last, zero if nxt is None else pltpu.roll(nxt[i], 127, 1), pltpu.roll(x[i], 127, 1))
            for i in range(NI)
        ]

    def left_of(x, prv):
        return [
            jnp.where(first, zero if prv is None else pltpu.roll(prv[i], 1, 1), pltpu.roll(x[i], 1, 1))
            for i in range(NI)
        ]

    def block(b, _):
        n = rows_s[b]
        info = [face_info(match_s, home_s, b, side, me, devices) for side in range(2)]
        for side in range(2):

            @pl.when(info[side][0] & (info[side][1] == 2 * core))
            def _():
                insert(U, G, Q, b, side, n, got_o)
                for k in range(3):
                    row = pl.ds(LO - 1 - k if side == 0 else LO + n + k, 1)
                    sides = SL[:, k : k + 1, :] + SR[:, k : k + 1, :]
                    X[b, WIDE, :, row, :] = got_o[0:NT, 4 + k : 5 + k, :] + sides
                    if k < 2:
                        for s in range(S):
                            m = 7 + 2 * s + k
                            X[b, LEFT + s, :, row, :] = SL[:, m : m + 1, :]
                            X[b, RIGHT + s, :, row, :] = SR[:, m : m + 1, :]

        lane_own = MID + B * core + b
        cr = CR[...]

        def pick(l):
            return jnp.sum(jnp.where(l8 == l, cr, 0.0), axis=1, keepdims=True)

        c_own = pick(lane_own)
        c_side = [pick(lane_own + i[5]) for i in info]
        lo = jnp.where(info[0][0], -4, 0)
        hi = jnp.where(info[1][0], n + 3, n - 1)
        w_in, w_edge, corr, alive, linked = [], [], [], [], []
        for i in range(NI):
            r = NI * s8 + (i - 4)
            inside = (r >= lo) & (r <= hi)
            wall = ((r == 0) & (lo == 0)) | ((r == n - 1) & (hi == n - 1))
            links = jnp.where(wall, 1.0, 2.0)
            w_in.append(jnp.where(inside, 0.8 / (2.5 + links), 0.0))
            w_edge.append(jnp.where(inside, 0.8 / (1.5 + links), 0.0))
            c = jnp.where(r < 0, c_side[0], jnp.where(r >= n, c_side[1], c_own))
            corr.append(jnp.where(inside, c, 0.0))
            alive.append((r >= 0) & (r < n))
            linked.append(jnp.where(((r == -1) & (lo == 0)) | ((r == n - 1) & (hi == n - 1)), 0.0, 1.0))

        def weight(i, j):
            if j == 0:
                return jnp.where(first, w_edge[i], w_in[i])
            if j == NT - 1:
                return jnp.where(last, w_edge[i], w_in[i])
            return w_in[i]

        for j in range(NT):
            cur = [G[b, j, at(i), :] for i in range(NI)]
            u, d = up(cur), down(cur)
            for i in range(NI):
                x = 0.2 * cur[i] + weight(i, j) * (X[b, WIDE, j, at(i), :] + (u[i] + d[i]))
                MIDS[i, j] = x + corr[i]
        prv, cur = None, [MIDS[i, 0] for i in range(NI)]
        for j in range(NT):
            nxt = [MIDS[i, j + 1] for i in range(NI)] if j < NT - 1 else None
            u, d, lf, rt = up(cur), down(cur), left_of(cur, prv), right_of(cur, nxt)
            for i in range(NI):
                q = Q[b, j, at(i), :]
                x = 0.2 * cur[i] + weight(i, j) * (q + ((u[i] + d[i]) + (lf[i] + rt[i])))
                G[b, j, at(i), :] = jnp.where(alive[i], x, 0.0)
                LV[0, i, j] = x
            prv, cur = cur, nxt
        for c in pot_copies(b):
            c.start()

        one = jnp.ones((8, 128), F32)
        edge_right, edge_left = jnp.where(last, 0.0, one), jnp.where(first, 0.0, one)
        prv, cur = None, [LV[0, i, 0] for i in range(NI)]
        for j in range(NT):
            nxt = [LV[0, i, j + 1] for i in range(NI)] if j < NT - 1 else None
            u, rt = up(cur), right_of(cur, nxt)
            m = edge_right if j == NT - 1 else one
            ml = edge_left if j == 0 else one
            step = [(0.5 * m) * (rt[i] - cur[i]) for i in range(NI)]
            past = left_of(step, prv)
            for i in range(NI):
                half = (0.5 * linked[i]) * (u[i] - cur[i])
                a, d = linked[i] + half, linked[i] - half
                LV[0, i, j], LV[1, i, j], LV[2, i, j], LV[3, i, j] = a, d, a + half, d - half
                a, d, al, dl = m + step[i], m - step[i], ml + past[i], ml - past[i]
                LH[0, i, j], LH[1, i, j], LH[2, i, j] = a, dl, d + al
                LH[3, i, j], LH[4, i, j], LH[5, i, j] = d, al, a + dl
                LH[6, i, j], LH[7, i, j] = a + step[i], dl - past[i]
                LH[8, i, j] = (d - step[i]) + (al + past[i])
            prv, cur = step, nxt

        def species(s, _):
            ia = jnp.where(s == 0, 0, jnp.where(s == 2, 2, 1))
            ib = jnp.where(s == 0, 1, jnp.where(s == 2, 3, 0))
            k1 = 0.1 * diff_s[s]
            k2 = 0.05 * diff_s[s]

            ih = jnp.where(s == 0, 0, jnp.where(s == 2, 6, 3))

            def rates(j, cur, lf, rt):
                u = up(cur)
                fv = [u[i] * LV[ia, i, j] - cur[i] * LV[ib, i, j] for i in range(NI)]
                fd = down(fv)
                fh = [
                    (rt[i] * LH[ih, i, j] + lf[i] * LH[ih + 1, i, j]) - cur[i] * LH[ih + 2, i, j]
                    for i in range(NI)
                ]
                return [(fv[i] - fd[i]) + fh[i] for i in range(NI)]

            for j in range(NT):
                cur, lf, rt = ([X[b, p + s, j, at(i), :] for i in range(NI)] for p in (0, LEFT, RIGHT))
                rate = rates(j, cur, lf, rt)
                for i in range(NI):
                    MIDS[i, j] = cur[i] + k1 * rate[i]
            prv, cur = None, [MIDS[i, 0] for i in range(NI)]
            for j in range(NT):
                nxt = [MIDS[i, j + 1] for i in range(NI)] if j < NT - 1 else None
                rate = rates(j, cur, left_of(cur, prv), right_of(cur, nxt))
                for i in range(NI):
                    x = 0.5 * (U[b, s, j, at(i), :] + cur[i]) + k2 * rate[i]
                    U[b, s, j, at(i), :] = jnp.where(alive[i], x, 0.0)
                prv, cur = cur, nxt
            for c in end_copies(b, s):
                c.start()
            return 0

        lax.fori_loop(0, S, species, 0, unroll=True)
        return 0

    lax.fori_loop(0, B, block, 0)
    for b in range(B):
        for c in pot_copies(b):
            c.wait()
        for s in range(S):
            for c in end_copies(b, s):
                c.wait()


HBM = pl.BlockSpec(memory_space=pltpu.HBM)
VMEM = pl.BlockSpec(memory_space=pltpu.VMEM)
def limit(mib):
    return pltpu.CompilerParams(vmem_limit_bytes=mib * 1024 * 1024)


def tables(devices):
    return pltpu.SMEM((B,), jnp.int32), pltpu.SMEM((devices * B,), jnp.int32), pltpu.SMEM((B, 2, 3), jnp.int32)


def shaped(*shape):
    return jax.ShapeDtypeStruct(shape, F32)


def body(concentration, potential_guess, diffusivity, block_rows, block_home, face_match):
    devices = lax.axis_size(AXIS)
    concentration, potential_guess, block_rows, block_home, face_match, diffusivity = (
        pltpu.with_memory_space_constraint(x, pltpu.HBM)
        for x in (concentration, potential_guess, block_rows, block_home, face_match, diffusivity)
    )

    def swap(x, pairs):
        return lax.ppermute(x, AXIS, pairs)

    on_chip = [(i, i ^ 1) for i in range(devices)]
    off_chip = [(i, (i + 1 if i % 2 else i - 1) % devices) for i in range(devices)]
    def beyond(k):
        return [((i + k if i % 2 else i - k) % devices, i) for i in range(devices)]


    state = pltpu.VMEM((B, PLANES, NT, H, 128), F32)
    message = pltpu.VMEM((NT + 1, 16, 128), F32)
    msg_e, msg_o, x = pl.pallas_call(
        functools.partial(pack_kernel, devices),
        out_shape=(message, message, state),
        in_specs=[HBM] * 5,
        out_specs=(VMEM,) * 3,
        scratch_shapes=[
            *tables(devices),
            pltpu.SemaphoreType.DMA((B,)),
            pltpu.SemaphoreType.DMA((3,)),
        ],
        compiler_params=limit(40),
        name="pack",
    )(concentration, potential_guess, block_rows, block_home, face_match)

    got_e = swap(msg_e, on_chip)
    record = pltpu.VMEM((FAR, 128), F32)
    chip = pl.pallas_call(
        chip_kernel,
        out_shape=record,
        in_specs=[VMEM, VMEM],
        out_specs=VMEM,
        compiler_params=limit(1),
        name="chip",
    )(msg_o, got_e)
    msg_o = pl.pallas_call(
        stamp_kernel,
        out_shape=message,
        in_specs=[VMEM, VMEM],
        out_specs=VMEM,
        input_output_aliases={0: 0},
        compiler_params=limit(1),
        name="stamp",
    )(msg_o, chip)
    third = swap(chip, beyond(6))
    second = swap(chip, beyond(4))
    x = pl.pallas_call(
        functools.partial(prep_kernel, devices),
        out_shape=state,
        in_specs=[VMEM] * 2 + [HBM] * 3,
        out_specs=VMEM,
        scratch_shapes=[*tables(devices), pltpu.SemaphoreType.DMA((3,))],
        input_output_aliases={0: 0},
        compiler_params=limit(40),
        name="prep",
    )(x, got_e, block_rows, block_home, face_match)
    got_o = swap(msg_o, off_chip)
    x, chip = lax.optimization_barrier((x, chip))
    w2 = pl.pallas_call(
        join_kernel,
        out_shape=pltpu.VMEM((8, 128), F32),
        in_specs=[VMEM] * 4,
        out_specs=VMEM,
        compiler_params=limit(1),
        name="join",
    )(chip, third, second, got_o)
    w_other = swap(w2, on_chip)

    out = pl.pallas_call(
        functools.partial(main_kernel, devices),
        out_shape=(shaped(B, S, ROWS, FACE), shaped(B, ROWS, FACE), state),
        in_specs=[VMEM] * 4 + [HBM] * 4,
        out_specs=(HBM, HBM, VMEM),
        scratch_shapes=[
            pltpu.VMEM((4, NI, NT, 8, 128), F32),
            pltpu.VMEM((9, NI, NT, 8, 128), F32),
            pltpu.VMEM((NI, NT, 8, 128), F32),
            pltpu.VMEM((8, 128), F32),
            pltpu.VMEM((NT, 16, 128), F32),
            pltpu.VMEM((NT, 16, 128), F32),
            *tables(devices),
            pltpu.SMEM((4,), F32),
            pltpu.SemaphoreType.DMA((B,)),
            pltpu.SemaphoreType.DMA((4,)),
        ],
        input_output_aliases={0: 2},
        compiler_params=limit(40),
        name="transport",
    )(x, w2, w_other, got_o, block_rows, block_home, face_match, diffusivity)
    return out[0], out[1]


def solution(mesh):
    in_specs = (
        P("blk", None, None, None),
        P("blk", None, None),
        P(),
        P("blk"),
        P(),
        P("blk", None, None),
    )
    out_specs = (P("blk", None, None, None), P("blk", None, None))
    return jax.shard_map(body, mesh=mesh, in_specs=in_specs, out_specs=out_specs, check_vma=False)
```
